32 devices in a mesh: stack: 2 (over x), scene: 16 (over z, y, core).
Axes of the slice: x: 2, y: 2, z: 4, core: 2. Of those that a mesh axis runs over, the one named last changes fastest.
Arguments:
- raw_echoes: bfloat16 [4096, 2, 4, 512], P('scene', None, 'stack'), parts along dimension 2, may hold values from -6 to 6
- azimuth_phase: float32 [8192, 512], P('stack', 'scene'), parts along dimension 0, may hold values from -3.140625 to 3.140625
- band_offset: int32 [1024], P(('stack', 'scene')), parts along dimension 0, may hold values from 0 to 8, as said below
- partners: int32 [2, 2], P('stack'), parts along dimension 0, may hold values from 0 to 0, as said below
Outputs:
- goldstein: bfloat16 [4, 1024, 2, 512], P('stack', None, None, 'scene'), parts along dimension 0
The draws below stay inside these ranges and needn't reach their ends.
There are 2 independent parts, one for each index of `stack`. The reference program is written for one: setup_inputs(seed, part) draws one part's arguments, and reference() takes and returns one part's arrays. A program takes and returns all parts, laid end to end along the dimension named above; each array names one. Nothing has to cross between parts.
Inputs may be any that keep to these rules, and one draw needn't show every extreme that they name: `partners`: row i names two dates that precede date i + 1, each from 0 to i, possibly equal; the last row's first entry is 0. `band_offset`: both 0 and 8 occur among the range bins.
All inputs are finite; a program needn't handle non-finite values.
Results may differ from the reference program's by a relative error of at most 0.023.
Values may be sent and summed in bfloat16 or wider, within the bound.
A program may use at most 128 MiB of HBM per device.

```python
import math
import jax
import jax.numpy as jnp
from jax import lax

AZ = 4096
SPLIT = 64
DATES = 2
LOOKS = 4
PATCH = 64
SHIFT = 8
RG = 512
PAIRS = 2


def draw_band_offset(key, part):
    first_key, second_key = jax.random.split(jax.random.fold_in(key, 11), 2)
    values = jax.random.randint(first_key, (RG,), 0, SHIFT + 1)
    spots = jax.random.permutation(second_key, RG)
    places = jnp.arange(RG, dtype=jnp.int32)
    values = jnp.where(places == spots[0], SHIFT, values)
    values = jnp.where(places == spots[1], 0, values)
    return values.astype(jnp.int32)


def draw_partners(key, part):
    noise = jax.random.randint(jax.random.fold_in(key, 23), (DATES - 1, 2), 0, 1 << 20)
    rows_index = jnp.arange(DATES - 1, dtype=jnp.int32)[:, None]
    cols_index = jnp.arange(2, dtype=jnp.int32)[None, :]
    picks = noise % (rows_index + 1)
    picks = jnp.where((rows_index == DATES - 2) & (cols_index == 0), DATES - 2, picks)
    return picks.astype(jnp.int32)


def levels(stream_key, extent, shards, least, largest):
    gain, own = 1.0, jax.random.fold_in(stream_key, 6)
    for dim, shards_of in shards:
        draws = jnp.exp(jax.random.uniform(jax.random.fold_in(own, dim), (shards_of,), jnp.float32, least / len(shards), largest / len(shards)))
        gain = gain * jnp.repeat(draws, extent[dim] // shards_of).reshape([-1 if axis == dim else 1 for axis in range(len(extent))])
    return gain


def centred(rng, shape, deviation, limit, shards=(), kind=jnp.bfloat16):
    factor_of = levels(rng, shape, shards, -0.22, 0.18) if shards else 1.0
    entries = jax.random.normal(rng, shape, jnp.float32) * deviation * factor_of
    return jnp.minimum(jnp.maximum(entries, -limit), limit).astype(kind)


def setup_inputs(seed: int = 0, part: int = 0) -> dict:
    seeds = jax.random.split(jax.random.key(seed), 5)
    own_keys = jax.random.split(jax.random.fold_in(seeds[4], part), 5)
    raw_echoes = centred(own_keys[0], (AZ, 2, DATES, RG), 1.0, 6.0, ((0, 16),))
    azimuth_phase = jnp.clip(jax.random.uniform(own_keys[1], (AZ, RG), jnp.float32, -3.140625, 3.140625), -3.140625, 3.140625)
    band_offset = draw_band_offset(jax.random.fold_in(jax.random.fold_in(seeds[4], part), 71), part)
    partners = draw_partners(jax.random.fold_in(jax.random.fold_in(seeds[4], part), 71), part)
    return {"raw_echoes": raw_echoes, "azimuth_phase": azimuth_phase, "band_offset": band_offset, "partners": partners}


epsilon = 1e-06

def dft_tables(size):
    position = jnp.arange(size, dtype=jnp.int32)
    phase_angle = (position[:, None] * position[None, :] % size).astype(jnp.float32) * (2.0 * math.pi / size)
    return (jnp.cos(phase_angle).astype(jnp.bfloat16), jnp.sin(phase_angle).astype(jnp.bfloat16))

def twiddles(size):
    position = jnp.arange(size, dtype=jnp.int32)
    phase_angle = (position[:, None] * position[None, :] % (size * size)).astype(jnp.float32) * (2.0 * math.pi / (size * size))
    return (jnp.cos(phase_angle), jnp.sin(phase_angle))

def dft_segment(cos_table, sin_table, data, pattern, direction):
    values = data.astype(jnp.float32)
    cos_part = jnp.einsum(pattern, cos_table.astype(jnp.float32), values, precision=lax.Precision.HIGHEST)
    sin_part = jnp.einsum(pattern, sin_table.astype(jnp.float32), values, precision=lax.Precision.HIGHEST)
    real_part = cos_part[:, :, 0] + direction * sin_part[:, :, 1]
    imag_part = cos_part[:, :, 1] - direction * sin_part[:, :, 0]
    return (real_part, imag_part)

def apply_twiddle(real_part, imag_part, direction):
    twist_cos, twist_sin = twiddles(SPLIT)
    tail_shape = (1,) * (real_part.ndim - 2)
    twist_cos = twist_cos.reshape(twist_cos.shape + tail_shape)
    twist_sin = twist_sin.reshape(twist_sin.shape + tail_shape)
    real_out = real_part * twist_cos + direction * imag_part * twist_sin
    imag_out = imag_part * twist_cos - direction * real_part * twist_sin
    return jnp.stack([real_out, imag_out], axis=2).astype(jnp.bfloat16)

def forward_azimuth(signal):
    cos_table, sin_table = dft_tables(SPLIT)
    grid_view = signal.reshape((SPLIT, SPLIT) + signal.shape[1:])
    real_part, imag_part = dft_segment(cos_table, sin_table, grid_view, 'kp,pqcdr->kqcdr', 1.0)
    segmented = apply_twiddle(real_part, imag_part, 1.0)
    real_part, imag_part = dft_segment(cos_table, sin_table, segmented, 'mq,kqcdr->kmcdr', 1.0)
    result = jnp.stack([real_part, imag_part], axis=2) * (1.0 / SPLIT)
    return result.astype(jnp.bfloat16).reshape(signal.shape)

def inverse_azimuth(spectrum):
    cos_table, sin_table = dft_tables(SPLIT)
    grid_view = spectrum.reshape((SPLIT, SPLIT) + spectrum.shape[1:])
    real_part, imag_part = dft_segment(cos_table, sin_table, grid_view, 'qm,kmcdr->kqcdr', -1.0)
    segmented = apply_twiddle(real_part, imag_part, -1.0)
    real_part, imag_part = dft_segment(cos_table, sin_table, segmented, 'pk,kqcdr->pqcdr', -1.0)
    result = jnp.stack([real_part, imag_part], axis=2) * (1.0 / SPLIT)
    return result.astype(jnp.bfloat16).reshape(spectrum.shape)

def doppler_order(phase_table):
    total_rows = phase_table.shape[0]
    return phase_table.reshape(SPLIT, SPLIT, phase_table.shape[1]).transpose(1, 0, 2).reshape(total_rows, phase_table.shape[1])

def migrate(doppler, band, phase_flat):
    total_rows = doppler.shape[0]
    strip_width = doppler.shape[3] - 2 * SHIFT
    flat_index = jnp.arange(total_rows, dtype=jnp.int32)
    natural = flat_index // SPLIT + SPLIT * (flat_index % SPLIT)
    signed = jnp.where(natural < total_rows // 2, natural, natural - total_rows).astype(jnp.float32)
    doppler_ratio = (signed / (total_rows / 2.0)) ** 2
    offset = band.astype(jnp.float32)[None, :] * (doppler_ratio[:, None] - 0.5)
    real_sum = jnp.zeros((total_rows,) + doppler.shape[2:3] + (strip_width,), jnp.float32)
    imag_sum = jnp.zeros((total_rows,) + doppler.shape[2:3] + (strip_width,), jnp.float32)
    for tap_index in range(2 * SHIFT):
        distance = tap_index - SHIFT - offset
        weight = jnp.where(jnp.abs(distance) < SHIFT / 2.0, jnp.sinc(distance) * jnp.cos(math.pi * distance / SHIFT) ** 2, 0.0)
        window = doppler[:, :, :, tap_index:tap_index + strip_width].astype(jnp.float32)
        real_sum = real_sum + weight[:, None, :] * window[:, 0]
        imag_sum = imag_sum + weight[:, None, :] * window[:, 1]
    cos_phase = jnp.cos(phase_flat)[:, None, :]
    sin_phase = jnp.sin(phase_flat)[:, None, :]
    real_out = real_sum * cos_phase - imag_sum * sin_phase
    imag_out = imag_sum * cos_phase + real_sum * sin_phase
    return jnp.stack([real_out, imag_out], axis=1).astype(jnp.bfloat16)

def interfere(leading, trailing):
    leading = leading.astype(jnp.float32)
    trailing = trailing.astype(jnp.float32)
    real_part = leading[:, 0] * trailing[:, 0] + leading[:, 1] * trailing[:, 1]
    imag_part = leading[:, 1] * trailing[:, 0] - leading[:, 0] * trailing[:, 1]
    product = jnp.stack([real_part, imag_part], axis=1)
    looked = product.reshape((product.shape[0] // LOOKS, LOOKS) + product.shape[1:]).mean(axis=1)
    return looked.astype(jnp.bfloat16)

def goldstein(pair_block):
    stride = PATCH // 2
    quarter = PATCH // 4
    padded = jnp.pad(pair_block, ((quarter, quarter), (0, 0), (0, 0)))
    rows_in = padded.shape[0] // stride
    cols_in = padded.shape[2] // stride
    tile_grid = padded.reshape(rows_in, stride, 2, cols_in, stride)
    tile_grid = jnp.concatenate([tile_grid[:-1], tile_grid[1:]], axis=1)
    tile_grid = jnp.concatenate([tile_grid[:, :, :, :-1], tile_grid[:, :, :, 1:]], axis=4)
    cos_table, sin_table = dft_tables(PATCH)
    real_part, imag_part = dft_segment(cos_table, sin_table, tile_grid, 'ku,iucjv->ikcjv', 1.0)
    segmented = jnp.stack([real_part, imag_part], axis=2).astype(jnp.bfloat16)
    real_part, imag_part = dft_segment(cos_table, sin_table, segmented, 'lv,ikcjv->ikcjl', 1.0)
    real_part = real_part * (1.0 / PATCH)
    imag_part = imag_part * (1.0 / PATCH)
    magnitude = jnp.sqrt(real_part * real_part + imag_part * imag_part + epsilon)
    row_sum = magnitude + jnp.roll(magnitude, 1, axis=1) + jnp.roll(magnitude, -1, axis=1)
    smooth = (row_sum + jnp.roll(row_sum, 1, axis=3) + jnp.roll(row_sum, -1, axis=3)) / 9.0
    mean_level = lax.optimization_barrier(jnp.mean(smooth, axis=(1, 3), keepdims=True))
    filter_gain = smooth / (mean_level + epsilon)
    spectrum = jnp.stack([real_part * filter_gain, imag_part * filter_gain], axis=2).astype(jnp.bfloat16)
    central_cos = cos_table[quarter:quarter + stride]
    central_sin = sin_table[quarter:quarter + stride]
    real_part, imag_part = dft_segment(central_cos, central_sin, spectrum, 'uk,ikcjl->iucjl', -1.0)
    segmented = jnp.stack([real_part, imag_part], axis=2).astype(jnp.bfloat16)
    real_part, imag_part = dft_segment(central_cos, central_sin, segmented, 'vl,iucjl->iucjv', -1.0)
    result = jnp.stack([real_part, imag_part], axis=2) * (1.0 / PATCH)
    return result.reshape(pair_block.shape[0], 2, -1).astype(jnp.bfloat16)

def reference(raw_echoes, azimuth_phase, band_offset, partners):
    date_count = raw_echoes.shape[2]
    phase_flat = doppler_order(azimuth_phase)
    quarter = PATCH // 4

    def focus_date(position):
        signal = lax.dynamic_index_in_dim(raw_echoes, position, 2, keepdims=True)
        padded = jnp.pad(signal, ((0, 0), (0, 0), (0, 0), (SHIFT, SHIFT)))
        doppler = forward_azimuth(padded)
        compressed = migrate(doppler, band_offset, phase_flat)
        return inverse_azimuth(compressed)[:, :, 0]
    focused = lax.map(focus_date, jnp.arange(date_count, dtype=jnp.int32))
    later_dates = jnp.repeat(jnp.arange(1, date_count, dtype=jnp.int32), 2)
    earlier_dates = partners.reshape(-1).astype(jnp.int32)

    def one_pair(position):
        leading = lax.dynamic_index_in_dim(focused, later_dates[position], 0, keepdims=False)
        trailing = lax.dynamic_index_in_dim(focused, earlier_dates[position], 0, keepdims=False)
        looked = interfere(leading, trailing)
        pair_block = jnp.pad(looked, ((0, 0), (0, 0), (quarter, quarter)))
        return goldstein(pair_block)
    return lax.map(one_pair, jnp.arange(PAIRS, dtype=jnp.int32))
```

```python
import math

import jax
import jax.numpy as jnp
import numpy as np
from jax import lax
from jax.experimental import pallas as pl
from jax.experimental.pallas import tpu as pltpu
from jax.sharding import PartitionSpec as P

SPLIT = 64
LOOKS = 4
PATCH = 64
SHIFT = 8
TAPS = 2 * SHIFT - 1
EPSILON = 1e-06
STRIP = 32
GROUPS = STRIP // 2
LANES = 2 * SPLIT
CHUNKS = STRIP // 4
HALO_CHUNKS = CHUNKS // 2
VMEM_LIMIT = 56 * 1024 * 1024


def base_tables():
    k = np.arange(64)
    angle = 2.0 * np.pi * ((k[:, None] * k[None, :]) % 64) / 64.0
    return np.cos(angle), np.sin(angle)


def twiddle_tables():
    k = np.arange(SPLIT)
    angle = 2.0 * np.pi * ((k[:, None] * k[None, :]) % (SPLIT * SPLIT)) / (SPLIT * SPLIT)
    return (
        np.tile(np.cos(angle), (1, 2)).astype(np.float32),
        np.tile(np.sin(angle), (1, 2)).astype(np.float32),
    )


def bf16(table):
    return jnp.asarray(np.asarray(table, np.float32), jnp.bfloat16)


def left_table(direction):
    c, s = base_tables()
    return np.block([[c, direction * s], [-direction * s, c]])


def right_table(direction):
    c, s = base_tables()
    eye = np.eye(2)
    return np.block(
        [
            [np.kron(eye, c), np.kron(eye, -direction * s)],
            [np.kron(eye, direction * s), np.kron(eye, c)],
        ]
    )


def look_table():
    table = np.zeros((4, 2, 2, SPLIT, 2, 4, 2, SPLIT // LOOKS))
    for g in range(4):
        for c in range(2):
            for rb in range(2):
                for q in range(SPLIT):
                    table[g, c, rb, q, rb, g, c, q // LOOKS] = 1.0 / LOOKS
    return table.reshape(4 * 2 * 2 * SPLIT, 2 * 4 * 2 * SPLIT // LOOKS)


def patch_azimuth_table():
    c, s = base_tables()
    table = np.zeros((4, 4, 2, 16, 4, 2, 64))
    for p in range(4):
        part_c, part_s = c[16 * p : 16 * p + 16], s[16 * p : 16 * p + 16]
        for r in range(4):
            table[p, r, 0, :, r, 0] = part_c
            table[p, r, 1, :, r, 0] = part_s
            table[p, r, 0, :, r, 1] = -part_s
            table[p, r, 1, :, r, 1] = part_c
    return table.reshape(512, 512)


def patch_range_table():
    c, s = base_tables()
    return np.concatenate([c, s], axis=1)


def back_azimuth_table():
    c, s = base_tables()
    c, s = c[:, 16:48], s[:, 16:48]
    table = np.zeros((4, 2, 64, 2, 4, 32))
    for i in range(4):
        table[i, 0, :, 0, i] = c
        table[i, 1, :, 0, i] = -s
        table[i, 0, :, 1, i] = s
        table[i, 1, :, 1, i] = c
    return table.reshape(512, 256)


def back_range_table():
    c, s = base_tables()
    c, s = c[16:48], s[16:48]
    return np.block([[c, -s], [s, c]])


def whole(count):
    return [pl.BlockSpec(memory_space=pltpu.VMEM)] * count


def dot(a, b):
    return jnp.dot(a, b, preferred_element_type=jnp.float32)


def weights_kernel(band_ref, phase_ref, weight_ref, cos_ref, sin_ref):
    g = pl.program_id(0)
    shape = (SPLIT, LANES)
    lane = lax.broadcasted_iota(jnp.int32, shape, 1)
    row = lax.broadcasted_iota(jnp.int32, shape, 0)
    k = row + SPLIT * (lane & (SPLIT - 1))
    total = SPLIT * SPLIT
    f = jnp.where(k < total // 2, k, k - total).astype(jnp.float32)
    ratio = f * (2.0 / total)
    band = jnp.where(lane < SPLIT, band_ref[g], band_ref[g + GROUPS]).astype(jnp.float32)
    s = band * (ratio * ratio - 0.5)
    n = jnp.floor(s + 0.5)
    y = s - n
    y2 = y * y
    pi = math.pi
    poly = -(pi**11) / 39916800.0
    for power, fact in ((9, 362880.0), (7, -5040.0), (5, 120.0), (3, -6.0), (1, 1.0)):
        poly = poly * y2 + (pi**power) / fact
    odd = n.astype(jnp.int32) & 1
    lobe = jnp.where(odd == 1, 1.0, -1.0) * (y * poly) * (1.0 / pi)
    cos_s = 0.5 * jnp.cos(s * (pi / 4.0))
    sin_s = 0.5 * jnp.sin(s * (pi / 4.0))
    for tap in range(TAPS):
        m = tap + 1 - SHIFT
        x = m - s
        sign = 1.0 if m % 2 == 0 else -1.0
        safe = jnp.where(x == 0.0, 1.0, x)
        sinc = jnp.where(x == 0.0, 1.0, (sign * lobe) / safe)
        window = 0.5 + math.cos(pi * m / 4.0) * cos_s + math.sin(pi * m / 4.0) * sin_s
        weight_ref[0, tap] = jnp.where(jnp.abs(x) < SHIFT / 2.0, sinc * window, 0.0)
    cos_ref[0] = jnp.cos(phase_ref[0])
    sin_ref[0] = jnp.sin(phase_ref[0])


def make_weights(band, phase):
    block = pl.BlockSpec((1, SPLIT, LANES), lambda g: (g, 0, 0))
    plane = jax.ShapeDtypeStruct((GROUPS, SPLIT, LANES), jnp.float32)
    return pl.pallas_call(
        weights_kernel,
        grid=(GROUPS,),
        in_specs=[pl.BlockSpec(memory_space=pltpu.SMEM), block],
        out_specs=[
            pl.BlockSpec((1, TAPS, SPLIT, LANES), lambda g: (g, 0, 0, 0)),
            block,
            block,
        ],
        out_shape=[jax.ShapeDtypeStruct((GROUPS, TAPS, SPLIT, LANES), jnp.float32), plane, plane],
        cost_estimate=pl.CostEstimate(
            flops=60_000_000, bytes_accessed=10_000_000, transcendentals=600_000
        ),
        name="weights",
    )(band, phase)


def forward_kernel(x_ref, left_ref, right_ref, tc_ref, ts_ref, dop_ref, up_ref, down_ref):
    low = lax.broadcasted_iota(jnp.int32, (SPLIT, LANES), 1) < SPLIT
    for d in range(dop_ref.shape[0]):

        def body(i, carry):
            for half in range(2):
                g = i + half * (GROUPS // 2)
                start = pl.multiple_of((d * GROUPS + g) * LANES, LANES)
                first = dot(left_ref[...], x_ref[:, pl.ds(start, LANES)])
                re, im = first[:SPLIT], first[SPLIT:]
                tc, ts = tc_ref[...], ts_ref[...]
                segment = jnp.concatenate([re * tc + im * ts, im * tc - re * ts], axis=1)
                second = dot(segment.astype(jnp.bfloat16), right_ref[...]) * (1.0 / SPLIT)
                dop_ref[d, g] = second.astype(jnp.bfloat16)
                re, im = second[:, :LANES], second[:, LANES:]
                if half == 0:
                    edge = jnp.where(low, re, pltpu.roll(im, SPLIT, 1))
                    down_ref[d, i] = edge.astype(jnp.bfloat16)
                else:
                    edge = jnp.where(low, pltpu.roll(re, SPLIT, 1), im)
                    up_ref[d, i] = edge.astype(jnp.bfloat16)
            return carry

        lax.fori_loop(0, GROUPS // 2, body, 0, unroll=2)


def forward(x, dates, left):
    edge = jax.ShapeDtypeStruct((dates, SHIFT, SPLIT, LANES), jnp.bfloat16)
    tc, ts = twiddle_tables()
    return pl.pallas_call(
        forward_kernel,
        in_specs=whole(5),
        out_specs=whole(3),
        out_shape=[
            jax.ShapeDtypeStruct((dates, GROUPS, SPLIT, 2 * LANES), jnp.bfloat16),
            edge,
            edge,
        ],
        compiler_params=pltpu.CompilerParams(vmem_limit_bytes=VMEM_LIMIT),
        name="forward",
    )(x, bf16(left), bf16(right_table(1.0)), jnp.asarray(tc), jnp.asarray(ts))


def focus_kernel(
    dop_ref, before_ref, after_ref, weight_ref, cos_ref, sin_ref,
    right_ref, left_ref, tc_ref, ts_ref, look_ref, out_ref, ext_ref, high_ref, low_ref,
):
    low = lax.broadcasted_iota(jnp.int32, (SPLIT, LANES), 1) < SPLIT
    dates = dop_ref.shape[0]
    for d in range(dates):

        def fill(i, carry):
            own = dop_ref[d, i].astype(jnp.float32)
            top = dop_ref[d, i + SHIFT].astype(jnp.float32)
            before = before_ref[d, i].astype(jnp.float32)
            after = after_ref[d, i].astype(jnp.float32)
            before_parts = (before, pltpu.roll(before, SPLIT, 1))
            after_parts = (pltpu.roll(after, SPLIT, 1), after)
            for c in range(2):
                mine = own[:, c * LANES : (c + 1) * LANES]
                upper = top[:, c * LANES : (c + 1) * LANES]
                ext_ref[d, c, i + SHIFT] = mine
                ext_ref[d, c, i + 2 * SHIFT] = upper
                ext_ref[d, c, i] = jnp.where(low, before_parts[c], pltpu.roll(upper, SPLIT, 1))
                ext_ref[d, c, i + 3 * SHIFT] = jnp.where(
                    low, pltpu.roll(mine, SPLIT, 1), after_parts[c]
                )
            return carry

        lax.fori_loop(0, SHIFT, fill, 0)

    def body(g, carry):
        parts = []
        for half in range(2):
            rows = pl.ds(half * (SPLIT // 2), SPLIT // 2)
            sums = [jnp.zeros((SPLIT // 2, LANES), jnp.float32) for _ in range(2 * dates)]
            for tap in range(TAPS):
                weight = weight_ref[g, tap, rows]
                for d in range(dates):
                    for c in range(2):
                        sums[2 * d + c] += weight * ext_ref[d, c, g + tap + 1, rows]
            cos_phase, sin_phase = cos_ref[g, rows], sin_ref[g, rows]
            parts.append(
                [
                    jnp.concatenate(
                        [
                            sums[2 * d] * cos_phase - sums[2 * d + 1] * sin_phase,
                            sums[2 * d + 1] * cos_phase + sums[2 * d] * sin_phase,
                        ],
                        axis=1,
                    ).astype(jnp.bfloat16)
                    for d in range(dates)
                ]
            )
        focused = []
        for d in range(dates):
            compressed = jnp.concatenate([parts[0][d], parts[1][d]], axis=0)
            first = dot(compressed, right_ref[...])
            re, im = first[:, :LANES], first[:, LANES:]
            tc, ts = tc_ref[...], ts_ref[...]
            segment = jnp.concatenate([re * tc - im * ts, im * tc + re * ts], axis=0)
            second = dot(left_ref[...], segment.astype(jnp.bfloat16)) * (1.0 / SPLIT)
            second = second.astype(jnp.bfloat16).astype(jnp.float32)
            focused.append((second[:SPLIT], second[SPLIT:]))
        (tr, ti), (lr, li) = focused
        product = jnp.concatenate([lr * tr + li * ti, li * tr - lr * ti], axis=1)
        high = product.astype(jnp.bfloat16)
        high_ref[g] = high
        low_ref[g] = (product - high.astype(jnp.float32)).astype(jnp.bfloat16)
        return carry

    lax.fori_loop(0, GROUPS, body, 0)
    for big in range(GROUPS // 4):
        high = jnp.concatenate([high_ref[4 * big + j] for j in range(4)], axis=1)
        rest = jnp.concatenate([low_ref[4 * big + j] for j in range(4)], axis=1)
        looked = dot(high, look_ref[...]) + dot(rest, look_ref[...])
        out_ref[big] = looked[:, :LANES].astype(jnp.bfloat16)
        out_ref[HALO_CHUNKS + big] = looked[:, LANES:].astype(jnp.bfloat16)


def focus(dop, before, after, weight, cos_phase, sin_phase):
    dates = dop.shape[0]
    tc, ts = twiddle_tables()
    return pl.pallas_call(
        focus_kernel,
        in_specs=whole(11),
        out_specs=pl.BlockSpec(memory_space=pltpu.VMEM),
        out_shape=jax.ShapeDtypeStruct((CHUNKS, SPLIT, LANES), jnp.bfloat16),
        scratch_shapes=[
            pltpu.VMEM((dates, 2, GROUPS + 2 * SHIFT, SPLIT, LANES), jnp.float32),
            pltpu.VMEM((GROUPS, SPLIT, 2 * LANES), jnp.bfloat16),
            pltpu.VMEM((GROUPS, SPLIT, 2 * LANES), jnp.bfloat16),
        ],
        compiler_params=pltpu.CompilerParams(vmem_limit_bytes=VMEM_LIMIT),
        name="focus",
    )(
        dop, before, after, weight, cos_phase, sin_phase,
        bf16(right_table(-1.0)), bf16(left_table(-1.0)),
        jnp.asarray(tc), jnp.asarray(ts), bf16(look_table()),
    )


def filter_kernel(
    own_ref, before_ref, after_ref, azimuth_ref, range_ref, back_azimuth_ref, back_range_ref,
    out_ref, line_ref, grid_ref,
):
    patches = SPLIT // 2
    line_ref[...] = jnp.zeros(line_ref.shape, jnp.float32)
    for j in range(HALO_CHUNKS):
        line_ref[j, pl.ds(1, SPLIT)] = before_ref[j].astype(jnp.float32)
        line_ref[HALO_CHUNKS + CHUNKS + j, pl.ds(1, SPLIT)] = after_ref[j].astype(jnp.float32)
    for j in range(CHUNKS):
        line_ref[HALO_CHUNKS + j, pl.ds(1, SPLIT)] = own_ref[j].astype(jnp.float32)

    def forward_lines(step, carry):
        rows = []
        for j in range(4):
            chunk = 4 * step + j
            rows.append(
                jnp.concatenate(
                    [line_ref[chunk, pl.ds(p, patches, stride=2)] for p in range(4)], axis=1
                )
            )
        lines = jnp.concatenate(rows, axis=0).astype(jnp.bfloat16)
        result = dot(lines, azimuth_ref[...]).astype(jnp.bfloat16).astype(jnp.float32)
        for j in range(4):
            for r in range(4):
                start = pl.multiple_of(((4 * step + j) * 4 + r) * patches, patches)
                grid_ref[pl.ds(start, patches)] = result[
                    j * patches : (j + 1) * patches, r * LANES : (r + 1) * LANES
                ]
        return carry

    lax.fori_loop(0, (2 * HALO_CHUNKS + CHUNKS) // 4, forward_lines, 0)
    sign = jnp.where(lax.broadcasted_iota(jnp.int32, (PATCH, LANES), 1) < PATCH, 1.0, -1.0)

    def filter_patches(step, carry):
        tiles = []
        for j in range(4):
            tile = grid_ref[pl.ds(4 * step + j, PATCH, stride=patches)]
            swapped = pltpu.roll(tile, PATCH, 1) * sign
            tiles.append(jnp.concatenate([tile, swapped], axis=0).astype(jnp.bfloat16))
        spectra = dot(range_ref[...], jnp.concatenate(tiles, axis=1)) * (1.0 / PATCH)
        kept = []
        for j in range(4):
            spectrum = spectra[:, j * LANES : (j + 1) * LANES]
            power = spectrum * spectrum
            magnitude = jnp.sqrt(power + pltpu.roll(power, PATCH, 1) + EPSILON)
            row_sum = (
                magnitude
                + pltpu.roll(magnitude, 1, 0)
                + pltpu.roll(magnitude, PATCH - 1, 0)
            )
            smooth = (row_sum + pltpu.roll(row_sum, 1, 1) + pltpu.roll(row_sum, LANES - 1, 1)) * (
                1.0 / 9.0
            )
            level = jnp.sum(jnp.sum(magnitude, axis=0, keepdims=True), axis=1, keepdims=True)
            level = level * (1.0 / (PATCH * LANES)) + EPSILON
            kept.append((spectrum * (smooth / level)).astype(jnp.bfloat16))
        back = dot(jnp.concatenate(kept, axis=1), back_azimuth_ref[...]).astype(jnp.bfloat16)
        stacked = jnp.concatenate([back[:, :LANES], back[:, LANES:]], axis=0)
        result = (dot(back_range_ref[...], stacked) * (1.0 / PATCH)).astype(jnp.bfloat16)
        start = pl.multiple_of(step * LANES, LANES)
        for pair in range(out_ref.shape[0]):
            out_ref[pair, :, pl.ds(start, LANES)] = result
        return carry

    lax.fori_loop(0, patches // 4, filter_patches, 0)


def filtered(own, before, after, pairs):
    looks = SPLIT * SPLIT // LOOKS
    return pl.pallas_call(
        filter_kernel,
        in_specs=whole(7),
        out_specs=pl.BlockSpec(memory_space=pltpu.VMEM),
        out_shape=jax.ShapeDtypeStruct((pairs, 2 * STRIP, looks), jnp.bfloat16),
        scratch_shapes=[
            pltpu.VMEM((2 * CHUNKS, SPLIT + 8, LANES), jnp.float32),
            pltpu.VMEM((PATCH * SPLIT // 2, LANES), jnp.float32),
        ],
        compiler_params=pltpu.CompilerParams(vmem_limit_bytes=VMEM_LIMIT),
        name="filter",
    )(
        own, before, after,
        bf16(patch_azimuth_table()), bf16(patch_range_table()),
        bf16(back_azimuth_table()), bf16(back_range_table()),
    )


def shifted(last, initial, axis):
    count = lax.axis_size(axis)
    up = [(i, i + 1) for i in range(count - 1)]
    down = [(j, i) for i, j in up]
    return lax.ppermute(last, axis, up), lax.ppermute(initial, axis, down)


def on_device(raw_echoes, azimuth_phase, band_offset, partners):
    scene = lax.axis_size("scene")
    dates = raw_echoes.shape[2]
    local = raw_echoes.shape[0] // SPLIT
    pairs = partners.size
    assert dates == 2 and raw_echoes.shape[3] == scene * STRIP
    pieces = raw_echoes.reshape(local, SPLIT, 2, dates, scene, 2, GROUPS)
    pieces = pieces.transpose(4, 2, 0, 3, 6, 5, 1).reshape(
        scene, 2 * local, dates * GROUPS * LANES
    )
    arrived = lax.all_to_all(pieces, "scene", split_axis=0, concat_axis=0, tiled=True)
    arrived = arrived.reshape(2 * SPLIT, dates * GROUPS * LANES)
    left = left_table(1.0).reshape(2 * SPLIT, 2, scene, local)
    left = left.transpose(0, 2, 1, 3).reshape(2 * SPLIT, 2 * SPLIT)
    phase = azimuth_phase.reshape(SPLIT, SPLIT, 2, GROUPS)
    phase = phase.transpose(3, 1, 2, 0).reshape(GROUPS, SPLIT, LANES)
    weight, cos_phase, sin_phase = make_weights(band_offset, phase)
    dop, last, initial = forward(arrived, dates, left)
    before, after = shifted(last, initial, "scene")
    looked = focus(dop, before, after, weight, cos_phase, sin_phase)
    before, after = shifted(looked[CHUNKS - HALO_CHUNKS :], looked[:HALO_CHUNKS], "scene")
    result = filtered(looked, before, after, pairs)
    return result.reshape(pairs, 2, STRIP, -1).transpose(0, 3, 1, 2)


def solution(mesh):
    return jax.shard_map(
        on_device,
        mesh=mesh,
        in_specs=(
            P("scene", None, "stack", None),
            P("stack", "scene"),
            P(("stack", "scene")),
            P("stack", None),
        ),
        out_specs=P("stack", None, None, "scene"),
        check_vma=False,
    )
```

```python
import math

import jax
import jax.numpy as jnp
import numpy as np
from jax import lax
from jax.experimental import pallas as pl
from jax.experimental.pallas import tpu as pltpu
from jax.sharding import PartitionSpec as P

SPLIT = 64
LOOKS = 4
PATCH = 64
SHIFT = 8
TAPS = 2 * SHIFT - 1
EPSILON = 1e-06
STRIP = 32
GROUPS = STRIP // 2
LANES = 2 * SPLIT
CHUNKS = STRIP // 4
HALO_CHUNKS = CHUNKS // 2
VMEM_LIMIT = 56 * 1024 * 1024


def base_tables():
    k = np.arange(64)
    angle = 2.0 * np.pi * ((k[:, None] * k[None, :]) % 64) / 64.0
    return np.cos(angle), np.sin(angle)


def twiddle_tables():
    k = np.arange(SPLIT)
    angle = 2.0 * np.pi * ((k[:, None] * k[None, :]) % (SPLIT * SPLIT)) / (SPLIT * SPLIT)
    return (
        np.tile(np.cos(angle), (1, 2)).astype(np.float32),
        np.tile(np.sin(angle), (1, 2)).astype(np.float32),
    )


def bf16(table):
    return jnp.asarray(np.asarray(table, np.float32), jnp.bfloat16)


def left_table(direction):
    c, s = base_tables()
    return np.block([[c, direction * s], [-direction * s, c]])


def right_table(direction):
    c, s = base_tables()
    eye = np.eye(2)
    return np.block(
        [
            [np.kron(eye, c), np.kron(eye, -direction * s)],
            [np.kron(eye, direction * s), np.kron(eye, c)],
        ]
    )


def look_table():
    table = np.zeros((4, 2, 2, SPLIT, 2, 4, 2, SPLIT // LOOKS))
    for g in range(4):
        for c in range(2):
            for rb in range(2):
                for q in range(SPLIT):
                    table[g, c, rb, q, rb, g, c, q // LOOKS] = 1.0 / LOOKS
    return table.reshape(4 * 2 * 2 * SPLIT, 2 * 4 * 2 * SPLIT // LOOKS)


def patch_azimuth_table():
    c, s = base_tables()
    table = np.zeros((4, 4, 2, 16, 4, 2, 64))
    for p in range(4):
        part_c, part_s = c[16 * p : 16 * p + 16], s[16 * p : 16 * p + 16]
        for r in range(4):
            table[p, r, 0, :, r, 0] = part_c
            table[p, r, 1, :, r, 0] = part_s
            table[p, r, 0, :, r, 1] = -part_s
            table[p, r, 1, :, r, 1] = part_c
    return table.reshape(512, 512)


def patch_range_table():
    c, s = base_tables()
    return np.concatenate([c, s], axis=1)


def back_azimuth_table():
    c, s = base_tables()
    c, s = c[:, 16:48], s[:, 16:48]
    table = np.zeros((4, 2, 64, 2, 4, 32))
    for i in range(4):
        table[i, 0, :, 0, i] = c
        table[i, 1, :, 0, i] = -s
        table[i, 0, :, 1, i] = s
        table[i, 1, :, 1, i] = c
    return table.reshape(512, 256)


def back_range_table():
    c, s = base_tables()
    c, s = c[16:48], s[16:48]
    return np.block([[c, -s], [s, c]])


def dot(a, b):
    return jnp.dot(a, b, preferred_element_type=jnp.float32)


def lane_order():
    lane = np.arange(SPLIT)
    return 2 * (lane % (SPLIT // 2)) + lane // (SPLIT // 2)


def spectrum_side(table, axis):
    order = np.concatenate([SPLIT * half + lane_order() for half in range(4)])
    return np.take(table, order, axis=axis)


def make_weights(g, band_ref, phase_ref, weight_ref, cos_ref, sin_ref):
    shape = (SPLIT, LANES)
    lane = lax.broadcasted_iota(jnp.int32, shape, 1)
    row = lax.broadcasted_iota(jnp.int32, shape, 0)
    half = SPLIT // 2
    k = row + SPLIT * (2 * (lane & (half - 1)) + ((lane & half) // half))
    total = SPLIT * SPLIT
    f = jnp.where(k < total // 2, k, k - total).astype(jnp.float32)
    ratio = f * (2.0 / total)
    band = jnp.where(lane < SPLIT, band_ref[g], band_ref[g + GROUPS]).astype(jnp.float32)
    s = band * (ratio * ratio - 0.5)
    n = jnp.floor(s + 0.5)
    y = s - n
    y2 = y * y
    pi = math.pi
    poly = -(pi**11) / 39916800.0
    for power, fact in ((9, 362880.0), (7, -5040.0), (5, 120.0), (3, -6.0), (1, 1.0)):
        poly = poly * y2 + (pi**power) / fact
    odd = n.astype(jnp.int32) & 1
    lobe = jnp.where(odd == 1, 1.0, -1.0) * (y * poly) * (1.0 / pi)
    cos_s = 0.5 * jnp.cos(s * (pi / 4.0))
    sin_s = 0.5 * jnp.sin(s * (pi / 4.0))
    for tap in range(TAPS):
        m = tap + 1 - SHIFT
        x = m - s
        sign = 1.0 if m % 2 == 0 else -1.0
        safe = jnp.where(x == 0.0, 1.0, x)
        sinc = jnp.where(x == 0.0, 1.0, (sign * lobe) / safe)
        window = 0.5 + math.cos(pi * m / 4.0) * cos_s + math.sin(pi * m / 4.0) * sin_s
        weight_ref[g, tap] = jnp.where(jnp.abs(x) < SHIFT / 2.0, sinc * window, 0.0)
    first, second = phase_ref[g], phase_ref[g + GROUPS]
    pieces = [first, pltpu.roll(first, SPLIT, 1), second, pltpu.roll(second, SPLIT, 1)]
    angle = jnp.concatenate(pieces, axis=0).T[:SPLIT]
    cos_ref[g] = jnp.cos(angle)
    sin_ref[g] = jnp.sin(angle)


def arrived_lines(wide_ref, g, sources, local, low):
    rows = []
    for c in range(2):
        for pair in range(wide_ref.shape[1]):
            one = wide_ref[c, pair, pl.ds(g, sources, stride=STRIP)]
            two = wide_ref[c, pair, pl.ds(g + GROUPS, sources, stride=STRIP)]
            rows.append(jnp.where(low[:sources], one, pltpu.roll(two, SPLIT, 1)))
            if local > 1:
                rows.append(jnp.where(low[:sources], pltpu.roll(one, SPLIT, 1), two))
    return jnp.concatenate(rows, axis=0).astype(jnp.bfloat16)


def scene_kernel(
    raw_ref, band_ref, phase_ref,
    left_ref, right_ref, back_right_ref, back_left_ref, tc_ref, ts_ref, look_ref,
    azimuth_ref, range_ref, back_azimuth_ref, back_range_ref,
    out_ref,
    recv_ref, wide_ref, weight_ref, cos_ref, sin_ref, ext_ref,
    up_ref, down_ref, before_ref, after_ref, high_ref, low_ref,
    own_ref, own_before_ref, own_after_ref, line_ref, grid_ref,
    send_sem, recv_sem, local_sem, edge_send, edge_recv, look_send, look_recv,
):
    scene = lax.axis_size("scene")
    me = lax.axis_index("scene")
    dates = raw_ref.shape[1]
    local = raw_ref.shape[3] // SPLIT
    low = lax.broadcasted_iota(jnp.int32, (SPLIT, LANES), 1) < SPLIT
    patches = SPLIT // 2

    barrier = pltpu.get_barrier_semaphore()

    def greet(o, carry):
        pl.semaphore_signal(
            barrier, inc=1, device_id={"scene": lax.rem(me + o, scene)},
            device_id_type=pl.DeviceIdType.MESH,
        )
        return carry

    lax.fori_loop(1, scene, greet, 0)
    pl.semaphore_wait(barrier, scene - 1)

    def strip_copy(d, o):
        peer = lax.rem(me + o, scene)
        start = pl.multiple_of(peer * STRIP, STRIP)
        return pltpu.make_async_remote_copy(
            src_ref=raw_ref.at[:, d, pl.ds(start, STRIP)],
            dst_ref=recv_ref.at[d, me],
            send_sem=send_sem.at[d, o],
            recv_sem=recv_sem.at[d, o],
            device_id={"scene": peer},
            device_id_type=pl.DeviceIdType.MESH,
        )

    def own_copy(d):
        start = pl.multiple_of(me * STRIP, STRIP)
        return pltpu.make_async_copy(
            raw_ref.at[:, d, pl.ds(start, STRIP)], recv_ref.at[d, me], local_sem.at[d]
        )

    for d in range(dates):

        def send(o, carry):
            strip_copy(d, o).start()
            return carry

        lax.fori_loop(1, scene, send, 0)
        own_copy(d).start()

    def weigh(g, carry):
        make_weights(g, band_ref, phase_ref, weight_ref, cos_ref, sin_ref)
        return carry

    lax.fori_loop(0, GROUPS, weigh, 0)

    @pl.when(me == 0)
    def _():
        before_ref[...] = jnp.zeros(before_ref.shape, before_ref.dtype)
        own_before_ref[...] = jnp.zeros(own_before_ref.shape, own_before_ref.dtype)

    @pl.when(me == scene - 1)
    def _():
        after_ref[...] = jnp.zeros(after_ref.shape, after_ref.dtype)
        own_after_ref[...] = jnp.zeros(own_after_ref.shape, own_after_ref.dtype)

    line_ref[...] = jnp.zeros(line_ref.shape, jnp.float32)

    def neighbour(source, target, send, recv, step):
        return pltpu.make_async_remote_copy(
            src_ref=source, dst_ref=target, send_sem=send, recv_sem=recv,
            device_id={"scene": me + step}, device_id_type=pl.DeviceIdType.MESH,
        )

    def edge_copies(d):
        return (
            neighbour(up_ref.at[d], before_ref.at[d], edge_send.at[d, 0], edge_recv.at[d, 0], 1),
            neighbour(down_ref.at[d], after_ref.at[d], edge_send.at[d, 1], edge_recv.at[d, 1], -1),
        )

    def look_copies():
        return (
            neighbour(
                own_ref.at[pl.ds(CHUNKS - HALO_CHUNKS, HALO_CHUNKS)], own_before_ref,
                look_send.at[0], look_recv.at[0], 1,
            ),
            neighbour(
                own_ref.at[pl.ds(0, HALO_CHUNKS)], own_after_ref,
                look_send.at[1], look_recv.at[1], -1,
            ),
        )

    def start_pair(copies):
        @pl.when(me < scene - 1)
        def _():
            copies[0].start()

        @pl.when(me > 0)
        def _():
            copies[1].start()

    def wait_pair(copies):
        @pl.when(me > 0)
        def _():
            copies[0].wait_recv()
            copies[1].wait_send()

        @pl.when(me < scene - 1)
        def _():
            copies[1].wait_recv()
            copies[0].wait_send()

    for d in range(dates):

        def arrive(o, carry):
            strip_copy(d, o).wait_recv()
            return carry

        lax.fori_loop(1, scene, arrive, 0)
        own_copy(d).wait()

        def widen(source, carry):
            start = pl.multiple_of(source * STRIP, STRIP)
            for c in range(2):
                strip = recv_ref[d, source, c].astype(jnp.float32)
                for pair in range(wide_ref.shape[1]):
                    part = strip[:, pair * LANES : (pair + 1) * LANES]
                    wide_ref[c, pair, pl.ds(start, STRIP), : part.shape[1]] = part
            return carry

        lax.fori_loop(0, scene, widen, 0)

        def forward(i, carry):
            for half in range(2):
                g = i + half * (GROUPS // 2)
                lines = arrived_lines(wide_ref, g, scene, local, low)
                first = dot(left_ref[...], lines)
                re, im = first[:SPLIT], first[SPLIT:]
                tc, ts = tc_ref[...], ts_ref[...]
                segment = jnp.concatenate([re * tc + im * ts, im * tc - re * ts], axis=1)
                second = dot(segment.astype(jnp.bfloat16), right_ref[...]) * (1.0 / SPLIT)
                second = second.astype(jnp.bfloat16).astype(jnp.float32)
                re, im = second[:, :LANES], second[:, LANES:]
                re_turned, im_turned = pltpu.roll(re, SPLIT, 1), pltpu.roll(im, SPLIT, 1)
                other = i + (0 if half else 3 * SHIFT)
                ext_ref[d, 0, g + SHIFT] = re
                ext_ref[d, 1, g + SHIFT] = im
                ext_ref[d, 0, other] = re_turned
                ext_ref[d, 1, other] = im_turned
                if half == 0:
                    down_ref[d, i] = jnp.where(low, re, im_turned).astype(jnp.bfloat16)
                else:
                    up_ref[d, i] = jnp.where(low, re_turned, im).astype(jnp.bfloat16)
            return carry

        lax.fori_loop(0, GROUPS // 2, forward, 0, unroll=2)
        start_pair(edge_copies(d))

    for d in range(dates):
        wait_pair(edge_copies(d))

        def fill(i, carry):
            before = before_ref[d, i].astype(jnp.float32)
            after = after_ref[d, i].astype(jnp.float32)
            before_parts = (before, pltpu.roll(before, SPLIT, 1))
            after_parts = (pltpu.roll(after, SPLIT, 1), after)
            for c in range(2):
                ext_ref[d, c, i] = jnp.where(low, before_parts[c], ext_ref[d, c, i])
                last = i + 3 * SHIFT
                ext_ref[d, c, last] = jnp.where(low, ext_ref[d, c, last], after_parts[c])
            return carry

        lax.fori_loop(0, SHIFT, fill, 0)

    def focus(g, carry):
        parts = []
        for half in range(2):
            rows = pl.ds(half * (SPLIT // 2), SPLIT // 2)
            sums = [jnp.zeros((SPLIT // 2, LANES), jnp.float32) for _ in range(2 * dates)]
            for tap in range(TAPS):
                weight = weight_ref[g, tap, rows]
                for d in range(dates):
                    for c in range(2):
                        sums[2 * d + c] += weight * ext_ref[d, c, g + tap + 1, rows]
            cos_phase, sin_phase = cos_ref[g, rows], sin_ref[g, rows]
            parts.append(
                [
                    jnp.concatenate(
                        [
                            sums[2 * d] * cos_phase - sums[2 * d + 1] * sin_phase,
                            sums[2 * d + 1] * cos_phase + sums[2 * d] * sin_phase,
                        ],
                        axis=1,
                    ).astype(jnp.bfloat16)
                    for d in range(dates)
                ]
            )
        focused = []
        for d in range(dates):
            compressed = jnp.concatenate([parts[0][d], parts[1][d]], axis=0)
            first = dot(compressed, back_right_ref[...])
            re, im = first[:, :LANES], first[:, LANES:]
            tc, ts = tc_ref[...], ts_ref[...]
            segment = jnp.concatenate([re * tc - im * ts, im * tc + re * ts], axis=0)
            second = dot(back_left_ref[...], segment.astype(jnp.bfloat16)) * (1.0 / SPLIT)
            second = second.astype(jnp.bfloat16).astype(jnp.float32)
            focused.append((second[:SPLIT], second[SPLIT:]))
        (tr, ti), (lr, li) = focused
        product = jnp.concatenate([lr * tr + li * ti, li * tr - lr * ti], axis=1)
        high = product.astype(jnp.bfloat16)
        high_ref[g] = high
        low_ref[g] = (product - high.astype(jnp.float32)).astype(jnp.bfloat16)
        return carry

    lax.fori_loop(0, GROUPS, focus, 0)
    for big in range(GROUPS // 4):
        high = jnp.concatenate([high_ref[4 * big + j] for j in range(4)], axis=1)
        rest = jnp.concatenate([low_ref[4 * big + j] for j in range(4)], axis=1)
        looked = dot(high, look_ref[...]) + dot(rest, look_ref[...])
        own_ref[big] = looked[:, :LANES].astype(jnp.bfloat16)
        own_ref[HALO_CHUNKS + big] = looked[:, LANES:].astype(jnp.bfloat16)
    start_pair(look_copies())

    def lines_of(first_chunk, count):
        def forward_lines(step, carry):
            rows = []
            for j in range(4):
                chunk = first_chunk + 4 * step + j
                rows.append(
                    jnp.concatenate(
                        [line_ref[chunk, pl.ds(p, patches, stride=2)] for p in range(4)], axis=1
                    )
                )
            lines = jnp.concatenate(rows, axis=0).astype(jnp.bfloat16)
            result = dot(lines, azimuth_ref[...]).astype(jnp.bfloat16).astype(jnp.float32)
            for j in range(4):
                for r in range(4):
                    start = ((first_chunk + 4 * step + j) * 4 + r) * patches
                    grid_ref[pl.ds(pl.multiple_of(start, patches), patches)] = result[
                        j * patches : (j + 1) * patches, r * LANES : (r + 1) * LANES
                    ]
            return carry

        lax.fori_loop(0, count // 4, forward_lines, 0)

    for j in range(CHUNKS):
        line_ref[HALO_CHUNKS + j, pl.ds(1, SPLIT)] = own_ref[j].astype(jnp.float32)
    lines_of(HALO_CHUNKS, CHUNKS)
    wait_pair(look_copies())
    for j in range(HALO_CHUNKS):
        line_ref[j, pl.ds(1, SPLIT)] = own_before_ref[j].astype(jnp.float32)
        line_ref[HALO_CHUNKS + CHUNKS + j, pl.ds(1, SPLIT)] = own_after_ref[j].astype(jnp.float32)
    lines_of(0, HALO_CHUNKS)
    lines_of(HALO_CHUNKS + CHUNKS, HALO_CHUNKS)
    sign = jnp.where(low, 1.0, -1.0)

    def filter_patches(step, carry):
        tiles = []
        for j in range(4):
            tile = grid_ref[pl.ds(4 * step + j, PATCH, stride=patches)]
            swapped = pltpu.roll(tile, PATCH, 1) * sign
            tiles.append(jnp.concatenate([tile, swapped], axis=0).astype(jnp.bfloat16))
        spectra = dot(range_ref[...], jnp.concatenate(tiles, axis=1)) * (1.0 / PATCH)
        kept = []
        for j in range(4):
            spectrum = spectra[:, j * LANES : (j + 1) * LANES]
            power = spectrum * spectrum
            magnitude = jnp.sqrt(power + pltpu.roll(power, PATCH, 1) + EPSILON)
            row_sum = (
                magnitude
                + pltpu.roll(magnitude, 1, 0)
                + pltpu.roll(magnitude, PATCH - 1, 0)
            )
            smooth = (row_sum + pltpu.roll(row_sum, 1, 1) + pltpu.roll(row_sum, LANES - 1, 1)) * (
                1.0 / 9.0
            )
            level = jnp.sum(jnp.sum(magnitude, axis=0, keepdims=True), axis=1, keepdims=True)
            level = level * (1.0 / (PATCH * LANES)) + EPSILON
            kept.append((spectrum * (smooth / level)).astype(jnp.bfloat16))
        back = dot(jnp.concatenate(kept, axis=1), back_azimuth_ref[...]).astype(jnp.bfloat16)
        stacked = jnp.concatenate([back[:, :LANES], back[:, LANES:]], axis=0)
        result = (dot(back_range_ref[...], stacked) * (1.0 / PATCH)).astype(jnp.bfloat16)
        start = pl.multiple_of(step * LANES, LANES)
        for pair in range(out_ref.shape[0]):
            out_ref[pair, :, pl.ds(start, LANES)] = result
        return carry

    lax.fori_loop(0, patches // 4, filter_patches, 0)

    for d in range(dates):

        def sent(o, carry):
            strip_copy(d, o).wait_send()
            return carry

        lax.fori_loop(1, scene, sent, 0)


def run_scene(raw, band, phase, left, scene, pairs):
    dates = raw.shape[1]
    width = raw.shape[3]
    looks = SPLIT * SPLIT // LOOKS
    tc, ts = twiddle_tables()
    vmem = pl.BlockSpec(memory_space=pltpu.VMEM)
    plane = (GROUPS, SPLIT, LANES)
    edge = pltpu.VMEM((dates, SHIFT, SPLIT, LANES), jnp.bfloat16)
    looked_edge = pltpu.VMEM((HALO_CHUNKS, SPLIT, LANES), jnp.bfloat16)
    products = pltpu.VMEM((GROUPS, SPLIT, 2 * LANES), jnp.bfloat16)
    dma = pltpu.SemaphoreType.DMA
    return pl.pallas_call(
        scene_kernel,
        in_specs=[pl.BlockSpec(memory_space=pl.ANY), pl.BlockSpec(memory_space=pltpu.SMEM)]
        + [vmem] * 12,
        out_specs=vmem,
        out_shape=jax.ShapeDtypeStruct((pairs, 2 * STRIP, looks), jnp.bfloat16),
        scratch_shapes=[
            pltpu.VMEM((dates, scene, 2, STRIP, width), jnp.bfloat16),
            pltpu.VMEM((2, pl.cdiv(width, LANES), scene * STRIP, LANES), jnp.float32),
            pltpu.VMEM((GROUPS, TAPS, SPLIT, LANES), jnp.float32),
            pltpu.VMEM(plane, jnp.float32),
            pltpu.VMEM(plane, jnp.float32),
            pltpu.VMEM((dates, 2, GROUPS + 2 * SHIFT, SPLIT, LANES), jnp.float32),
            edge, edge, edge, edge, products, products,
            pltpu.VMEM((CHUNKS, SPLIT, LANES), jnp.bfloat16),
            looked_edge,
            looked_edge,
            pltpu.VMEM((2 * CHUNKS, SPLIT + 8, LANES), jnp.float32),
            pltpu.VMEM((PATCH * SPLIT // 2, LANES), jnp.float32),
            dma((dates, scene)), dma((dates, scene)), dma((dates,)),
            dma((dates, 2)), dma((dates, 2)), dma((2,)), dma((2,)),
        ],
        compiler_params=pltpu.CompilerParams(
            vmem_limit_bytes=VMEM_LIMIT, collective_id=0, has_side_effects=True
        ),
        name="scene",
    )(
        raw, band, phase, bf16(left), bf16(spectrum_side(right_table(1.0), 1)),
        bf16(spectrum_side(right_table(-1.0), 0)), bf16(left_table(-1.0)),
        jnp.asarray(tc), jnp.asarray(ts), bf16(look_table()),
        bf16(patch_azimuth_table()), bf16(patch_range_table()),
        bf16(back_azimuth_table()), bf16(back_range_table()),
    )


def on_device(raw_echoes, azimuth_phase, band_offset, partners):
    scene = lax.axis_size("scene")
    dates = raw_echoes.shape[2]
    local = raw_echoes.shape[0] // SPLIT
    pairs = partners.size
    assert dates == 2 and raw_echoes.shape[3] == scene * STRIP
    left = left_table(1.0).reshape(2 * SPLIT, 2, scene, local)
    left = left.transpose(0, 1, 3, 2).reshape(2 * SPLIT, 2 * SPLIT)
    raw = raw_echoes.transpose(1, 2, 3, 0)
    phase = azimuth_phase.T.reshape(STRIP, SPLIT // 2, LANES)
    result = run_scene(raw, band_offset, phase, left, scene, pairs)
    return result.reshape(pairs, 2, STRIP, -1).transpose(0, 3, 1, 2)


def solution(mesh):
    return jax.shard_map(
        on_device,
        mesh=mesh,
        in_specs=(
            P("scene", None, "stack", None),
            P("stack", "scene"),
            P(("stack", "scene")),
            P("stack", None),
        ),
        out_specs=P("stack", None, None, "scene"),
        check_vma=False,
    )
```

```python
import math

import jax
import jax.numpy as jnp
import numpy as np
from jax import lax
from jax.experimental import pallas as pl
from jax.experimental.pallas import tpu as pltpu
from jax.sharding import PartitionSpec as P

SPLIT = 64
LOOKS = 4
PATCH = 64
SHIFT = 8
TAPS = 2 * SHIFT - 1
EPSILON = 1e-06
STRIP = 32
GROUPS = STRIP // 2
LANES = 2 * SPLIT
CHUNKS = STRIP // 4
HALO_CHUNKS = CHUNKS // 2
TABLES = 13
VMEM_LIMIT = 56 * 1024 * 1024


def base_tables():
    k = np.arange(64)
    angle = 2.0 * np.pi * ((k[:, None] * k[None, :]) % 64) / 64.0
    return np.cos(angle), np.sin(angle)


def twiddle_tables():
    k = np.arange(SPLIT)
    angle = 2.0 * np.pi * ((k[:, None] * k[None, :]) % (SPLIT * SPLIT)) / (SPLIT * SPLIT)
    return (
        np.tile(np.cos(angle), (1, 2)).astype(np.float32),
        np.tile(np.sin(angle), (1, 2)).astype(np.float32),
    )


def bf16(table):
    return jnp.asarray(np.asarray(table, np.float32), jnp.bfloat16)


def left_table(direction):
    c, s = base_tables()
    return np.block([[c, direction * s], [-direction * s, c]])


def right_table(direction):
    c, s = base_tables()
    eye = np.eye(2)
    return np.block(
        [
            [np.kron(eye, c), np.kron(eye, -direction * s)],
            [np.kron(eye, direction * s), np.kron(eye, c)],
        ]
    )


def look_table():
    table = np.zeros((4, 2, 2, SPLIT, 2, 4, 2, SPLIT // LOOKS))
    for g in range(4):
        for c in range(2):
            for rb in range(2):
                for q in range(SPLIT):
                    table[g, c, rb, q, rb, g, c, q // LOOKS] = 1.0 / LOOKS
    return table.reshape(4 * 2 * 2 * SPLIT, 2 * 4 * 2 * SPLIT // LOOKS)


def patch_azimuth_table():
    c, s = base_tables()
    table = np.zeros((4, 4, 2, 16, 4, 2, 64))
    for p in range(4):
        part_c, part_s = c[16 * p : 16 * p + 16], s[16 * p : 16 * p + 16]
        for r in range(4):
            table[p, r, 0, :, r, 0] = part_c
            table[p, r, 1, :, r, 0] = part_s
            table[p, r, 0, :, r, 1] = -part_s
            table[p, r, 1, :, r, 1] = part_c
    return table.reshape(512, 512)


def patch_range_table():
    c, s = base_tables()
    return np.concatenate([c, s], axis=1)


def back_azimuth_table():
    c, s = base_tables()
    c, s = c[:, 16:48], s[:, 16:48]
    table = np.zeros((4, 2, 64, 2, 4, 32))
    for i in range(4):
        table[i, 0, :, 0, i] = c
        table[i, 1, :, 0, i] = -s
        table[i, 0, :, 1, i] = s
        table[i, 1, :, 1, i] = c
    return table.reshape(512, 256)


def back_range_table():
    c, s = base_tables()
    c, s = c[16:48], s[16:48]
    return np.block([[c, -s], [s, c]])


def dot(a, b):
    return jnp.dot(a, b, preferred_element_type=jnp.float32)


def lane_order():
    lane = np.arange(SPLIT)
    return 2 * (lane % (SPLIT // 2)) + lane // (SPLIT // 2)


def spectrum_side(table, axis):
    order = np.concatenate([SPLIT * half + lane_order() for half in range(4)])
    return np.take(table, order, axis=axis)


def cos_sin(angle):
    h = 0.5 * angle
    h2 = h * h
    sin_h = 1.0 / 6227020800.0
    for fact in (-39916800.0, 362880.0, -5040.0, 120.0, -6.0, 1.0):
        sin_h = sin_h * h2 + 1.0 / fact
    sin_h = sin_h * h
    cos_h = 1.0 / 479001600.0
    for fact in (-3628800.0, 40320.0, -720.0, 24.0, -2.0, 1.0):
        cos_h = cos_h * h2 + 1.0 / fact
    return 1.0 - 2.0 * sin_h * sin_h, 2.0 * sin_h * cos_h


def make_weights(g, band_ref, lines_ref, weight_ref, cos_ref, sin_ref):
    shape = (SPLIT, LANES)
    lane = lax.broadcasted_iota(jnp.int32, shape, 1)
    row = lax.broadcasted_iota(jnp.int32, shape, 0)
    half = SPLIT // 2
    k = row + SPLIT * (2 * (lane & (half - 1)) + ((lane & half) // half))
    total = SPLIT * SPLIT
    f = jnp.where(k < total // 2, k, k - total).astype(jnp.float32)
    ratio = f * (2.0 / total)
    band = jnp.where(lane < SPLIT, band_ref[g], band_ref[g + GROUPS]).astype(jnp.float32)
    s = band * (ratio * ratio - 0.5)
    n = jnp.floor(s + 0.5)
    y = s - n
    y2 = y * y
    pi = math.pi
    poly = -(pi**11) / 39916800.0
    for power, fact in ((9, 362880.0), (7, -5040.0), (5, 120.0), (3, -6.0), (1, 1.0)):
        poly = poly * y2 + (pi**power) / fact
    odd = n.astype(jnp.int32) & 1
    lobe = jnp.where(odd == 1, 1.0, -1.0) * (y * poly) * (1.0 / pi)
    cos_s, sin_s = cos_sin(s * (pi / 4.0))
    cos_s, sin_s = 0.5 * cos_s, 0.5 * sin_s
    for tap in range(TAPS):
        m = tap + 1 - SHIFT
        x = m - s
        sign = 1.0 if m % 2 == 0 else -1.0
        safe = jnp.where(x == 0.0, 1.0, x)
        sinc = jnp.where(x == 0.0, 1.0, (sign * lobe) / safe)
        window = 0.5 + math.cos(pi * m / 4.0) * cos_s + math.sin(pi * m / 4.0) * sin_s
        weight_ref[g, tap] = jnp.where(jnp.abs(x) < SHIFT / 2.0, sinc * window, 0.0)
    first = lines_ref[pl.ds(g, SPLIT // 2, stride=STRIP)]
    second = lines_ref[pl.ds(g + GROUPS, SPLIT // 2, stride=STRIP)]
    pieces = [first, pltpu.roll(first, SPLIT, 1), second, pltpu.roll(second, SPLIT, 1)]
    angle = jnp.concatenate(pieces, axis=0).T[:SPLIT]
    cos_ref[g], sin_ref[g] = cos_sin(angle)


def arrived_lines(wide_ref, g, sources, local, low):
    rows = []
    for c in range(2):
        for pair in range(wide_ref.shape[1]):
            one = wide_ref[c, pair, pl.ds(g, sources, stride=STRIP)]
            two = wide_ref[c, pair, pl.ds(g + GROUPS, sources, stride=STRIP)]
            rows.append(jnp.where(low[:sources], one, pltpu.roll(two, SPLIT, 1)))
            if local > 1:
                rows.append(jnp.where(low[:sources], pltpu.roll(one, SPLIT, 1), two))
    return jnp.concatenate(rows, axis=0).astype(jnp.bfloat16)


def scene_kernel(
    band_ref, packed_ref, phase_ref,
    left_ref, right_ref, back_right_ref, back_left_ref, tc_ref, ts_ref, look_ref,
    azimuth_ref, range_ref, back_azimuth_ref, back_range_ref,
    out_ref,
    raw_ref, spread_ref, recv_ref, lines_ref, wide_ref, weight_ref, cos_ref, sin_ref, ext_ref,
    up_ref, down_ref, before_ref, after_ref, focused_ref, high_ref, low_ref,
    own_ref, own_before_ref, own_after_ref, line_ref, grid_ref,
    send_sem, recv_sem, local_sem, edge_send, edge_recv, look_send, look_recv,
    loads,
):
    scene = lax.axis_size("scene")
    me = lax.axis_index("scene")
    dates = raw_ref.shape[1]
    local = raw_ref.shape[3] // SPLIT
    low = lax.broadcasted_iota(jnp.int32, (SPLIT, LANES), 1) < SPLIT
    patches = SPLIT // 2

    barrier = pltpu.get_barrier_semaphore()

    def greet(o, carry):
        pl.semaphore_signal(
            barrier, inc=1, device_id={"scene": lax.rem(me + o, scene)},
            device_id_type=pl.DeviceIdType.MESH,
        )
        return carry

    lax.fori_loop(1, scene, greet, 0)
    for load in loads:
        load.start()
    loads[0].wait()
    height = packed_ref.shape[0]
    piece = height // 8

    def spread(i, carry):
        rows = pl.ds(pl.multiple_of(i * piece, piece), piece)
        spread_ref[rows] = packed_ref[rows].astype(jnp.float32)
        return carry

    lax.fori_loop(0, 8, spread, 0)
    tiles = raw_ref.shape[2] // LANES
    stride = 2 * tiles * dates

    def turn(d):
        def body(tile, carry):
            for c in range(2):
                start = (c * tiles + tile) * dates + d
                lines = spread_ref[pl.ds(start, raw_ref.shape[3], stride=stride)]
                target = pl.ds(pl.multiple_of(tile * LANES, LANES), LANES)
                raw_ref[c, d, target] = lines.T.astype(jnp.bfloat16)
            return carry

        lax.fori_loop(0, tiles, body, 0)

    turn(0)
    pl.semaphore_wait(barrier, scene - 1)

    def strip_copy(d, o):
        peer = lax.rem(me + o, scene)
        start = pl.multiple_of(peer * STRIP, STRIP)
        return pltpu.make_async_remote_copy(
            src_ref=raw_ref.at[:, d, pl.ds(start, STRIP)],
            dst_ref=recv_ref.at[d, me],
            send_sem=send_sem.at[d, o],
            recv_sem=recv_sem.at[d, o],
            device_id={"scene": peer},
            device_id_type=pl.DeviceIdType.MESH,
        )

    def own_copy(d):
        start = pl.multiple_of(me * STRIP, STRIP)
        return pltpu.make_async_copy(
            raw_ref.at[:, d, pl.ds(start, STRIP)], recv_ref.at[d, me], local_sem.at[d]
        )

    held = scene - scene // 3

    for d in range(dates):

        def send(o, carry):
            strip_copy(d, o).start()
            return carry

        if d:
            turn(d)
        lax.fori_loop(1, held if d else scene, send, 0)
        own_copy(d).start()

    for load in loads[1:]:
        load.wait()

    for part in range(SPLIT // 2):
        lines_ref[pl.ds(part * STRIP, STRIP)] = phase_ref[:, part * LANES : (part + 1) * LANES]

    def weigh(g, carry):
        make_weights(g, band_ref, lines_ref, weight_ref, cos_ref, sin_ref)
        return carry

    lax.fori_loop(0, GROUPS, weigh, 0)

    @pl.when(me == 0)
    def _():
        before_ref[...] = jnp.zeros(before_ref.shape, before_ref.dtype)
        own_before_ref[...] = jnp.zeros(own_before_ref.shape, own_before_ref.dtype)

    @pl.when(me == scene - 1)
    def _():
        after_ref[...] = jnp.zeros(after_ref.shape, after_ref.dtype)
        own_after_ref[...] = jnp.zeros(own_after_ref.shape, own_after_ref.dtype)

    line_ref[...] = jnp.zeros(line_ref.shape, jnp.float32)

    def neighbour(source, target, send, recv, step):
        return pltpu.make_async_remote_copy(
            src_ref=source, dst_ref=target, send_sem=send, recv_sem=recv,
            device_id={"scene": me + step}, device_id_type=pl.DeviceIdType.MESH,
        )

    def edge_copies(d):
        return (
            neighbour(up_ref.at[d], before_ref.at[d], edge_send.at[d, 0], edge_recv.at[d, 0], 1),
            neighbour(down_ref.at[d], after_ref.at[d], edge_send.at[d, 1], edge_recv.at[d, 1], -1),
        )

    def look_copies():
        return (
            neighbour(
                own_ref.at[pl.ds(CHUNKS - HALO_CHUNKS, HALO_CHUNKS)], own_before_ref,
                look_send.at[0], look_recv.at[0], 1,
            ),
            neighbour(
                own_ref.at[pl.ds(0, HALO_CHUNKS)], own_after_ref,
                look_send.at[1], look_recv.at[1], -1,
            ),
        )

    def start_pair(copies):
        @pl.when(me < scene - 1)
        def _():
            copies[0].start()

        @pl.when(me > 0)
        def _():
            copies[1].start()

    def wait_pair(copies):
        @pl.when(me > 0)
        def _():
            copies[0].wait_recv()
            copies[1].wait_send()

        @pl.when(me < scene - 1)
        def _():
            copies[1].wait_recv()
            copies[0].wait_send()

    def focus_date(d):
        wait_pair(edge_copies(d))

        def fill(i, carry):
            before = before_ref[d, i].astype(jnp.float32)
            after = after_ref[d, i].astype(jnp.float32)
            before_parts = (before, pltpu.roll(before, SPLIT, 1))
            after_parts = (pltpu.roll(after, SPLIT, 1), after)
            for c in range(2):
                ext_ref[d, c, i] = jnp.where(low, before_parts[c], ext_ref[d, c, i])
                last = i + 3 * SHIFT
                ext_ref[d, c, last] = jnp.where(low, ext_ref[d, c, last], after_parts[c])
            return carry

        lax.fori_loop(0, SHIFT, fill, 0, unroll=2)

        def focus(g, carry):
            re_sum = jnp.zeros((SPLIT, LANES), jnp.float32)
            im_sum = jnp.zeros((SPLIT, LANES), jnp.float32)
            for tap in range(TAPS):
                weight = weight_ref[g, tap]
                re_sum += weight * ext_ref[d, 0, g + tap + 1]
                im_sum += weight * ext_ref[d, 1, g + tap + 1]
            cos_phase, sin_phase = cos_ref[g], sin_ref[g]
            compressed = jnp.concatenate(
                [re_sum * cos_phase - im_sum * sin_phase, im_sum * cos_phase + re_sum * sin_phase],
                axis=1,
            ).astype(jnp.bfloat16)
            first = dot(compressed, back_right_ref[...])
            re, im = first[:, :LANES], first[:, LANES:]
            tc, ts = tc_ref[...], ts_ref[...]
            segment = jnp.concatenate([re * tc - im * ts, im * tc + re * ts], axis=0)
            second = dot(back_left_ref[...], segment.astype(jnp.bfloat16)) * (1.0 / SPLIT)
            second = second.astype(jnp.bfloat16)
            if d == 0:
                focused_ref[g] = second
                return carry
            leading, trailing = second.astype(jnp.float32), focused_ref[g].astype(jnp.float32)
            lr, li = leading[:SPLIT], leading[SPLIT:]
            tr, ti = trailing[:SPLIT], trailing[SPLIT:]
            product = jnp.concatenate([lr * tr + li * ti, li * tr - lr * ti], axis=1)
            high = product.astype(jnp.bfloat16)
            high_ref[g] = high
            low_ref[g] = (product - high.astype(jnp.float32)).astype(jnp.bfloat16)
            return carry

        lax.fori_loop(0, GROUPS, focus, 0, unroll=2)

    for d in range(dates):

        def arrive(o, carry):
            strip_copy(d, o).wait_recv()
            return carry

        lax.fori_loop(1, scene, arrive, 0)
        own_copy(d).wait()

        def widen(source, carry):
            start = pl.multiple_of(source * STRIP, STRIP)
            for c in range(2):
                strip = recv_ref[d, source, c].astype(jnp.float32)
                for pair in range(wide_ref.shape[1]):
                    part = strip[:, pair * LANES : (pair + 1) * LANES]
                    wide_ref[c, pair, pl.ds(start, STRIP), : part.shape[1]] = part
            return carry

        lax.fori_loop(0, scene, widen, 0)

        def forward(i, carry):
            for half in range(2):
                g = i + half * (GROUPS // 2)
                lines = arrived_lines(wide_ref, g, scene, local, low)
                first = dot(left_ref[...], lines)
                re, im = first[:SPLIT], first[SPLIT:]
                tc, ts = tc_ref[...], ts_ref[...]
                segment = jnp.concatenate([re * tc + im * ts, im * tc - re * ts], axis=1)
                second = dot(segment.astype(jnp.bfloat16), right_ref[...]) * (1.0 / SPLIT)
                second = second.astype(jnp.bfloat16).astype(jnp.float32)
                re, im = second[:, :LANES], second[:, LANES:]
                re_turned, im_turned = pltpu.roll(re, SPLIT, 1), pltpu.roll(im, SPLIT, 1)
                other = i + (0 if half else 3 * SHIFT)
                ext_ref[d, 0, g + SHIFT] = re
                ext_ref[d, 1, g + SHIFT] = im
                ext_ref[d, 0, other] = re_turned
                ext_ref[d, 1, other] = im_turned
                if half == 0:
                    down_ref[d, i] = jnp.where(low, re, im_turned).astype(jnp.bfloat16)
                else:
                    up_ref[d, i] = jnp.where(low, re_turned, im).astype(jnp.bfloat16)
            return carry

        lax.fori_loop(0, GROUPS // 2, forward, 0, unroll=2)
        start_pair(edge_copies(d))
        if d == 0:

            def send_rest(o, carry):
                strip_copy(1, o).start()
                return carry

            lax.fori_loop(held, scene, send_rest, 0)
        focus_date(d)

    for big in range(GROUPS // 4):
        high = jnp.concatenate([high_ref[4 * big + j] for j in range(4)], axis=1)
        rest = jnp.concatenate([low_ref[4 * big + j] for j in range(4)], axis=1)
        looked = dot(high, look_ref[...]) + dot(rest, look_ref[...])
        own_ref[big] = looked[:, :LANES].astype(jnp.bfloat16)
        own_ref[HALO_CHUNKS + big] = looked[:, LANES:].astype(jnp.bfloat16)
    start_pair(look_copies())

    def lines_of(first_chunk, count):
        def forward_lines(step, carry):
            rows = []
            for j in range(4):
                chunk = first_chunk + 4 * step + j
                rows.append(
                    jnp.concatenate(
                        [line_ref[chunk, pl.ds(p, patches, stride=2)] for p in range(4)], axis=1
                    )
                )
            lines = jnp.concatenate(rows, axis=0).astype(jnp.bfloat16)
            result = dot(lines, azimuth_ref[...]).astype(jnp.bfloat16).astype(jnp.float32)
            for j in range(4):
                for r in range(4):
                    start = ((first_chunk + 4 * step + j) * 4 + r) * patches
                    grid_ref[pl.ds(pl.multiple_of(start, patches), patches)] = result[
                        j * patches : (j + 1) * patches, r * LANES : (r + 1) * LANES
                    ]
            return carry

        lax.fori_loop(0, count // 4, forward_lines, 0)

    for j in range(CHUNKS):
        line_ref[HALO_CHUNKS + j, pl.ds(1, SPLIT)] = own_ref[j].astype(jnp.float32)
    lines_of(HALO_CHUNKS, CHUNKS)
    wait_pair(look_copies())
    for j in range(HALO_CHUNKS):
        line_ref[j, pl.ds(1, SPLIT)] = own_before_ref[j].astype(jnp.float32)
        line_ref[HALO_CHUNKS + CHUNKS + j, pl.ds(1, SPLIT)] = own_after_ref[j].astype(jnp.float32)
    lines_of(0, HALO_CHUNKS)
    lines_of(HALO_CHUNKS + CHUNKS, HALO_CHUNKS)
    sign = jnp.where(low, 1.0, -1.0)

    def filter_patches(step, carry):
        tiles = []
        for j in range(4):
            tile = grid_ref[pl.ds(4 * step + j, PATCH, stride=patches)]
            swapped = pltpu.roll(tile, PATCH, 1) * sign
            tiles.append(jnp.concatenate([tile, swapped], axis=0).astype(jnp.bfloat16))
        spectra = dot(range_ref[...], jnp.concatenate(tiles, axis=1)) * (1.0 / PATCH)
        kept = []
        for j in range(4):
            spectrum = spectra[:, j * LANES : (j + 1) * LANES]
            power = spectrum * spectrum
            magnitude = jnp.sqrt(power + pltpu.roll(power, PATCH, 1) + EPSILON)
            row_sum = (
                magnitude
                + pltpu.roll(magnitude, 1, 0)
                + pltpu.roll(magnitude, PATCH - 1, 0)
            )
            smooth = (row_sum + pltpu.roll(row_sum, 1, 1) + pltpu.roll(row_sum, LANES - 1, 1)) * (
                1.0 / 9.0
            )
            level = jnp.sum(jnp.sum(magnitude, axis=0, keepdims=True), axis=1, keepdims=True)
            level = level * (1.0 / (PATCH * LANES)) + EPSILON
            kept.append((spectrum * (smooth / level)).astype(jnp.bfloat16))
        back = dot(jnp.concatenate(kept, axis=1), back_azimuth_ref[...]).astype(jnp.bfloat16)
        stacked = jnp.concatenate([back[:, :LANES], back[:, LANES:]], axis=0)
        result = (dot(back_range_ref[...], stacked) * (1.0 / PATCH)).astype(jnp.bfloat16)
        start = pl.multiple_of(step * LANES, LANES)
        out_ref[:, pl.ds(start, LANES)] = result
        return carry

    lax.fori_loop(0, patches // 4, filter_patches, 0)

    for d in range(dates):

        def sent(o, carry):
            strip_copy(d, o).wait_send()
            return carry

        lax.fori_loop(1, scene, sent, 0)


def loading_kernel(band_ref, *refs):
    held, out_ref, kept, load_sem = refs[:TABLES], refs[TABLES], refs[TABLES + 1 : -1], refs[-1]
    loads = [
        pltpu.make_async_copy(source, target, load_sem.at[i])
        for i, (source, target) in enumerate(zip(held, kept[:TABLES]))
    ]
    scene_kernel(band_ref, *kept[:TABLES], out_ref, *kept[TABLES:], loads)


def run_scene(raw, band, phase, left, scene, shape):
    dates, width = shape[1], shape[3]
    looks = SPLIT * SPLIT // LOOKS
    tc, ts = twiddle_tables()
    vmem = pl.BlockSpec(memory_space=pltpu.VMEM)
    plane = (GROUPS, SPLIT, LANES)
    edge = pltpu.VMEM((dates, SHIFT, SPLIT, LANES), jnp.bfloat16)
    looked_edge = pltpu.VMEM((HALO_CHUNKS, SPLIT, LANES), jnp.bfloat16)
    products = pltpu.VMEM((GROUPS, SPLIT, 2 * LANES), jnp.bfloat16)
    dma = pltpu.SemaphoreType.DMA
    tables = (
        raw, phase, bf16(left), bf16(spectrum_side(right_table(1.0), 1)),
        bf16(spectrum_side(right_table(-1.0), 0)), bf16(left_table(-1.0)),
        jnp.asarray(tc), jnp.asarray(ts), bf16(look_table()),
        bf16(patch_azimuth_table()), bf16(patch_range_table()),
        bf16(back_azimuth_table()), bf16(back_range_table()),
    )
    return pl.pallas_call(
        loading_kernel,
        in_specs=[pl.BlockSpec(memory_space=pltpu.SMEM)]
        + [pl.BlockSpec(memory_space=pl.ANY)] * TABLES,
        out_specs=vmem,
        out_shape=jax.ShapeDtypeStruct((2 * STRIP, looks), jnp.bfloat16),
        scratch_shapes=[pltpu.VMEM(table.shape, table.dtype) for table in tables]
        + [
            pltpu.VMEM(shape, jnp.bfloat16),
            pltpu.VMEM(raw.shape, jnp.float32),
            pltpu.VMEM((dates, scene, 2, STRIP, width), jnp.bfloat16),
            pltpu.VMEM((STRIP * SPLIT // 2, LANES), jnp.float32),
            pltpu.VMEM((2, pl.cdiv(width, LANES), scene * STRIP, LANES), jnp.float32),
            pltpu.VMEM((GROUPS, TAPS, SPLIT, LANES), jnp.float32),
            pltpu.VMEM(plane, jnp.float32),
            pltpu.VMEM(plane, jnp.float32),
            pltpu.VMEM((dates, 2, GROUPS + 2 * SHIFT, SPLIT, LANES), jnp.float32),
            edge, edge, edge, edge,
            pltpu.VMEM((GROUPS, 2 * SPLIT, LANES), jnp.bfloat16),
            products, products,
            pltpu.VMEM((CHUNKS, SPLIT, LANES), jnp.bfloat16),
            looked_edge,
            looked_edge,
            pltpu.VMEM((2 * CHUNKS, SPLIT + 8, LANES), jnp.float32),
            pltpu.VMEM((PATCH * SPLIT // 2, LANES), jnp.float32),
            dma((dates, scene)), dma((dates, scene)), dma((dates,)),
            dma((dates, 2)), dma((dates, 2)), dma((2,)), dma((2,)), dma((TABLES,)),
        ],
        compiler_params=pltpu.CompilerParams(
            vmem_limit_bytes=VMEM_LIMIT, collective_id=0, has_side_effects=True
        ),
        name="scene",
    )(band, *tables)


def on_device(raw_echoes, azimuth_phase, band_offset, partners):
    scene = lax.axis_size("scene")
    dates = raw_echoes.shape[2]
    local = raw_echoes.shape[0] // SPLIT
    pairs = partners.size
    assert dates == 2 and raw_echoes.shape[3] == scene * STRIP
    left = left_table(1.0).reshape(2 * SPLIT, 2, scene, local)
    left = left.transpose(0, 1, 3, 2).reshape(2 * SPLIT, 2 * SPLIT)
    lines, bins = raw_echoes.shape[0], raw_echoes.shape[3]
    raw = raw_echoes.reshape(lines, 2, dates, bins // LANES, LANES)
    raw = raw.transpose(0, 1, 3, 2, 4).reshape(-1, LANES)
    phase = azimuth_phase.T
    result = run_scene(
        raw, band_offset, phase, left, scene, (2, dates, bins, lines)
    )
    result = jnp.broadcast_to(result, (pairs,) + result.shape)
    return result.reshape(pairs, 2, STRIP, -1).transpose(0, 3, 1, 2)


def solution(mesh):
    return jax.shard_map(
        on_device,
        mesh=mesh,
        in_specs=(
            P("scene", None, "stack", None),
            P("stack", "scene"),
            P(("stack", "scene")),
            P("stack", None),
        ),
        out_specs=P("stack", None, None, "scene"),
        check_vma=False,
    )
```

```python
import math

import jax
import jax.numpy as jnp
import numpy as np
from jax import lax
from jax.experimental import pallas as pl
from jax.experimental.pallas import tpu as pltpu
from jax.sharding import PartitionSpec as P

SPLIT = 64
LOOKS = 4
PATCH = 64
SHIFT = 8
TAPS = 2 * SHIFT - 1
EPSILON = 1e-06
STRIP = 32
GROUPS = STRIP // 2
LANES = 2 * SPLIT
CHUNKS = STRIP // 4
HALO_CHUNKS = CHUNKS // 2
TABLES = 13
VMEM_LIMIT = 56 * 1024 * 1024


def base_tables():
    k = np.arange(64)
    angle = 2.0 * np.pi * ((k[:, None] * k[None, :]) % 64) / 64.0
    return np.cos(angle), np.sin(angle)


def twiddle_tables():
    k = np.arange(SPLIT)
    angle = 2.0 * np.pi * ((k[:, None] * k[None, :]) % (SPLIT * SPLIT)) / (SPLIT * SPLIT)
    return (
        np.tile(np.cos(angle), (1, 2)).astype(np.float32),
        np.tile(np.sin(angle), (1, 2)).astype(np.float32),
    )


def bf16(table):
    return jnp.asarray(np.asarray(table, np.float32), jnp.bfloat16)


def left_table(direction):
    c, s = base_tables()
    return np.block([[c, direction * s], [-direction * s, c]])


def right_table(direction):
    c, s = base_tables()
    eye = np.eye(2)
    return np.block(
        [
            [np.kron(eye, c), np.kron(eye, -direction * s)],
            [np.kron(eye, direction * s), np.kron(eye, c)],
        ]
    )


def look_table():
    table = np.zeros((4, 2, 2, SPLIT, 2, 4, 2, SPLIT // LOOKS))
    for g in range(4):
        for c in range(2):
            for rb in range(2):
                for q in range(SPLIT):
                    table[g, c, rb, q, rb, g, c, q // LOOKS] = 1.0 / LOOKS
    return table.reshape(4 * 2 * 2 * SPLIT, 2 * 4 * 2 * SPLIT // LOOKS)


def patch_azimuth_table():
    c, s = base_tables()
    table = np.zeros((4, 4, 2, 16, 4, 2, 64))
    for p in range(4):
        part_c, part_s = c[16 * p : 16 * p + 16], s[16 * p : 16 * p + 16]
        for r in range(4):
            table[p, r, 0, :, r, 0] = part_c
            table[p, r, 1, :, r, 0] = part_s
            table[p, r, 0, :, r, 1] = -part_s
            table[p, r, 1, :, r, 1] = part_c
    return table.reshape(512, 512)


def patch_range_table():
    c, s = base_tables()
    return np.concatenate([c, s], axis=1)


def back_azimuth_table():
    c, s = base_tables()
    c, s = c[:, 16:48], s[:, 16:48]
    table = np.zeros((4, 2, 64, 2, 4, 32))
    for i in range(4):
        table[i, 0, :, 0, i] = c
        table[i, 1, :, 0, i] = -s
        table[i, 0, :, 1, i] = s
        table[i, 1, :, 1, i] = c
    return table.reshape(512, 256)


def back_range_table():
    c, s = base_tables()
    c, s = c[16:48], s[16:48]
    return np.block([[c, -s], [s, c]])


def dot(a, b):
    return jnp.dot(a, b, preferred_element_type=jnp.float32)


def lane_order():
    lane = np.arange(SPLIT)
    return 2 * (lane % (SPLIT // 2)) + lane // (SPLIT // 2)


def spectrum_side(table, axis):
    order = np.concatenate([SPLIT * half + lane_order() for half in range(4)])
    return np.take(table, order, axis=axis)


def cos_sin(angle):
    h = 0.5 * angle
    h2 = h * h
    sin_h = 1.0 / 6227020800.0
    for fact in (-39916800.0, 362880.0, -5040.0, 120.0, -6.0, 1.0):
        sin_h = sin_h * h2 + 1.0 / fact
    sin_h = sin_h * h
    cos_h = 1.0 / 479001600.0
    for fact in (-3628800.0, 40320.0, -720.0, 24.0, -2.0, 1.0):
        cos_h = cos_h * h2 + 1.0 / fact
    return 1.0 - 2.0 * sin_h * sin_h, 2.0 * sin_h * cos_h


def make_weights(g, band_ref, lines_ref, weight_ref, cos_ref, sin_ref):
    shape = (SPLIT, LANES)
    lane = lax.broadcasted_iota(jnp.int32, shape, 1)
    row = lax.broadcasted_iota(jnp.int32, shape, 0)
    half = SPLIT // 2
    k = row + SPLIT * (2 * (lane & (half - 1)) + ((lane & half) // half))
    total = SPLIT * SPLIT
    f = jnp.where(k < total // 2, k, k - total).astype(jnp.float32)
    ratio = f * (2.0 / total)
    band = jnp.where(lane < SPLIT, band_ref[g], band_ref[g + GROUPS]).astype(jnp.float32)
    s = band * (ratio * ratio - 0.5)
    n = jnp.floor(s + 0.5)
    y = s - n
    y2 = y * y
    pi = math.pi
    poly = -(pi**11) / 39916800.0
    for power, fact in ((9, 362880.0), (7, -5040.0), (5, 120.0), (3, -6.0), (1, 1.0)):
        poly = poly * y2 + (pi**power) / fact
    odd = n.astype(jnp.int32) & 1
    lobe = jnp.where(odd == 1, 1.0, -1.0) * (y * poly) * (1.0 / pi)
    cos_s, sin_s = cos_sin(s * (pi / 4.0))
    cos_s, sin_s = 0.5 * cos_s, 0.5 * sin_s
    for tap in range(TAPS):
        m = tap + 1 - SHIFT
        x = m - s
        sign = 1.0 if m % 2 == 0 else -1.0
        safe = jnp.where(x == 0.0, 1.0, x)
        sinc = jnp.where(x == 0.0, 1.0, (sign * lobe) / safe)
        window = 0.5 + math.cos(pi * m / 4.0) * cos_s + math.sin(pi * m / 4.0) * sin_s
        weight_ref[g, tap] = jnp.where(jnp.abs(x) < SHIFT / 2.0, sinc * window, 0.0)
    first = lines_ref[pl.ds(g, SPLIT // 2, stride=STRIP)]
    second = lines_ref[pl.ds(g + GROUPS, SPLIT // 2, stride=STRIP)]
    pieces = [first, pltpu.roll(first, SPLIT, 1), second, pltpu.roll(second, SPLIT, 1)]
    angle = jnp.concatenate(pieces, axis=0).T[:SPLIT]
    cos_ref[g], sin_ref[g] = cos_sin(angle)


def arrived_lines(wide_ref, g, sources, local, low):
    rows = []
    for c in range(2):
        for pair in range(wide_ref.shape[1]):
            one = wide_ref[c, pair, pl.ds(g, sources, stride=STRIP)]
            two = wide_ref[c, pair, pl.ds(g + GROUPS, sources, stride=STRIP)]
            rows.append(jnp.where(low[:sources], one, pltpu.roll(two, SPLIT, 1)))
            if local > 1:
                rows.append(jnp.where(low[:sources], pltpu.roll(one, SPLIT, 1), two))
    return jnp.concatenate(rows, axis=0).astype(jnp.bfloat16)


def scene_kernel(
    band_ref, packed_ref, phase_ref,
    left_ref, right_ref, back_right_ref, back_left_ref, tc_ref, ts_ref, look_ref,
    azimuth_ref, range_ref, back_azimuth_ref, back_range_ref,
    out_ref,
    raw_ref, spread_ref, recv_ref, lines_ref, wide_ref, weight_ref, cos_ref, sin_ref, ext_ref,
    up_ref, down_ref, before_ref, after_ref, focused_ref, high_ref, low_ref,
    own_ref, own_before_ref, own_after_ref, line_ref, grid_ref,
    send_sem, recv_sem, local_sem, edge_send, edge_recv, look_send, look_recv,
    loads,
):
    scene = lax.axis_size("scene")
    me = lax.axis_index("scene")
    dates = raw_ref.shape[1]
    local = raw_ref.shape[3] // SPLIT
    low = lax.broadcasted_iota(jnp.int32, (SPLIT, LANES), 1) < SPLIT
    patches = SPLIT // 2

    barrier = pltpu.get_barrier_semaphore()

    def greet(o, carry):
        pl.semaphore_signal(
            barrier, inc=1, device_id={"scene": lax.rem(me + o, scene)},
            device_id_type=pl.DeviceIdType.MESH,
        )
        return carry

    lax.fori_loop(1, scene, greet, 0)
    for load in loads:
        load.start()
    loads[0].wait()
    height = packed_ref.shape[0]
    piece = height // 8

    def spread(i, carry):
        rows = pl.ds(pl.multiple_of(i * piece, piece), piece)
        spread_ref[rows] = packed_ref[rows].astype(jnp.float32)
        return carry

    lax.fori_loop(0, 8, spread, 0)
    tiles = raw_ref.shape[2] // LANES
    stride = 2 * tiles * dates

    def turn(d):
        def body(tile, carry):
            for c in range(2):
                start = (c * tiles + tile) * dates + d
                lines = spread_ref[pl.ds(start, raw_ref.shape[3], stride=stride)]
                target = pl.ds(pl.multiple_of(tile * LANES, LANES), LANES)
                raw_ref[c, d, target] = lines.T.astype(jnp.bfloat16)
            return carry

        lax.fori_loop(0, tiles, body, 0)

    turn(0)
    pl.semaphore_wait(barrier, scene - 1)

    def strip_copy(d, o):
        peer = lax.rem(me + o, scene)
        start = pl.multiple_of(peer * STRIP, STRIP)
        return pltpu.make_async_remote_copy(
            src_ref=raw_ref.at[:, d, pl.ds(start, STRIP)],
            dst_ref=recv_ref.at[d, me],
            send_sem=send_sem.at[d, o],
            recv_sem=recv_sem.at[d, o],
            device_id={"scene": peer},
            device_id_type=pl.DeviceIdType.MESH,
        )

    def own_copy(d):
        start = pl.multiple_of(me * STRIP, STRIP)
        return pltpu.make_async_copy(
            raw_ref.at[:, d, pl.ds(start, STRIP)], recv_ref.at[d, me], local_sem.at[d]
        )

    held = scene - scene // 3

    for d in range(dates):

        def send(o, carry):
            strip_copy(d, o).start()
            return carry

        if d:
            turn(d)
        lax.fori_loop(1, held if d else scene, send, 0)
        own_copy(d).start()

    for load in loads[1:]:
        load.wait()

    for part in range(SPLIT // 2):
        lines_ref[pl.ds(part * STRIP, STRIP)] = phase_ref[:, part * LANES : (part + 1) * LANES]

    def weigh(g, carry):
        make_weights(g, band_ref, lines_ref, weight_ref, cos_ref, sin_ref)
        return carry

    lax.fori_loop(0, GROUPS, weigh, 0)

    @pl.when(me == 0)
    def _():
        before_ref[...] = jnp.zeros(before_ref.shape, before_ref.dtype)
        own_before_ref[...] = jnp.zeros(own_before_ref.shape, own_before_ref.dtype)

    @pl.when(me == scene - 1)
    def _():
        after_ref[...] = jnp.zeros(after_ref.shape, after_ref.dtype)
        own_after_ref[...] = jnp.zeros(own_after_ref.shape, own_after_ref.dtype)

    line_ref[...] = jnp.zeros(line_ref.shape, jnp.float32)

    def neighbour(source, target, send, recv, step):
        return pltpu.make_async_remote_copy(
            src_ref=source, dst_ref=target, send_sem=send, recv_sem=recv,
            device_id={"scene": me + step}, device_id_type=pl.DeviceIdType.MESH,
        )

    def edge_copies(d):
        return (
            neighbour(up_ref.at[d], before_ref.at[d], edge_send.at[d, 0], edge_recv.at[d, 0], 1),
            neighbour(down_ref.at[d], after_ref.at[d], edge_send.at[d, 1], edge_recv.at[d, 1], -1),
        )

    def look_copies():
        return (
            neighbour(
                own_ref.at[pl.ds(CHUNKS - HALO_CHUNKS, HALO_CHUNKS)], own_before_ref,
                look_send.at[0], look_recv.at[0], 1,
            ),
            neighbour(
                own_ref.at[pl.ds(0, HALO_CHUNKS)], own_after_ref,
                look_send.at[1], look_recv.at[1], -1,
            ),
        )

    def start_pair(copies):
        @pl.when(me < scene - 1)
        def _():
            copies[0].start()

        @pl.when(me > 0)
        def _():
            copies[1].start()

    def wait_pair(copies):
        @pl.when(me > 0)
        def _():
            copies[0].wait_recv()
            copies[1].wait_send()

        @pl.when(me < scene - 1)
        def _():
            copies[1].wait_recv()
            copies[0].wait_send()

    def focus_date(d):
        wait_pair(edge_copies(d))

        def fill(i, carry):
            before = before_ref[d, i].astype(jnp.float32)
            after = after_ref[d, i].astype(jnp.float32)
            before_parts = (before, pltpu.roll(before, SPLIT, 1))
            after_parts = (pltpu.roll(after, SPLIT, 1), after)
            for c in range(2):
                ext_ref[d, c, i] = jnp.where(low, before_parts[c], ext_ref[d, c, i])
                last = i + 3 * SHIFT
                ext_ref[d, c, last] = jnp.where(low, ext_ref[d, c, last], after_parts[c])
            return carry

        lax.fori_loop(0, SHIFT, fill, 0, unroll=2)

        def focus(g, carry):
            re_sum = jnp.zeros((SPLIT, LANES), jnp.float32)
            im_sum = jnp.zeros((SPLIT, LANES), jnp.float32)
            for tap in range(TAPS):
                weight = weight_ref[g, tap]
                re_sum += weight * ext_ref[d, 0, g + tap + 1]
                im_sum += weight * ext_ref[d, 1, g + tap + 1]
            cos_phase, sin_phase = cos_ref[g], sin_ref[g]
            compressed = jnp.concatenate(
                [re_sum * cos_phase - im_sum * sin_phase, im_sum * cos_phase + re_sum * sin_phase],
                axis=1,
            ).astype(jnp.bfloat16)
            first = dot(compressed, back_right_ref[...])
            re, im = first[:, :LANES], first[:, LANES:]
            tc, ts = tc_ref[...], ts_ref[...]
            segment = jnp.concatenate([re * tc - im * ts, im * tc + re * ts], axis=0)
            second = dot(back_left_ref[...], segment.astype(jnp.bfloat16)) * (1.0 / SPLIT)
            second = second.astype(jnp.bfloat16)
            if d == 0:
                focused_ref[g] = second
                return carry
            leading, trailing = second.astype(jnp.float32), focused_ref[g].astype(jnp.float32)
            lr, li = leading[:SPLIT], leading[SPLIT:]
            tr, ti = trailing[:SPLIT], trailing[SPLIT:]
            product = jnp.concatenate([lr * tr + li * ti, li * tr - lr * ti], axis=1)
            high = product.astype(jnp.bfloat16)
            high_ref[g] = high
            low_ref[g] = (product - high.astype(jnp.float32)).astype(jnp.bfloat16)
            return carry

        lax.fori_loop(0, GROUPS, focus, 0, unroll=8)

    for d in range(dates):

        def arrive(o, carry):
            strip_copy(d, o).wait_recv()
            return carry

        lax.fori_loop(1, scene, arrive, 0)
        own_copy(d).wait()

        def widen(source, carry):
            start = pl.multiple_of(source * STRIP, STRIP)
            for c in range(2):
                strip = recv_ref[d, source, c].astype(jnp.float32)
                for pair in range(wide_ref.shape[1]):
                    part = strip[:, pair * LANES : (pair + 1) * LANES]
                    wide_ref[c, pair, pl.ds(start, STRIP), : part.shape[1]] = part
            return carry

        lax.fori_loop(0, scene, widen, 0)

        def forward(i, carry):
            for half in range(2):
                g = i + half * (GROUPS // 2)
                lines = arrived_lines(wide_ref, g, scene, local, low)
                first = dot(left_ref[...], lines)
                re, im = first[:SPLIT], first[SPLIT:]
                tc, ts = tc_ref[...], ts_ref[...]
                segment = jnp.concatenate([re * tc + im * ts, im * tc - re * ts], axis=1)
                second = dot(segment.astype(jnp.bfloat16), right_ref[...]) * (1.0 / SPLIT)
                second = second.astype(jnp.bfloat16).astype(jnp.float32)
                re, im = second[:, :LANES], second[:, LANES:]
                re_turned, im_turned = pltpu.roll(re, SPLIT, 1), pltpu.roll(im, SPLIT, 1)
                other = i + (0 if half else 3 * SHIFT)
                ext_ref[d, 0, g + SHIFT] = re
                ext_ref[d, 1, g + SHIFT] = im
                ext_ref[d, 0, other] = re_turned
                ext_ref[d, 1, other] = im_turned
                if half == 0:
                    down_ref[d, i] = jnp.where(low, re, im_turned).astype(jnp.bfloat16)
                else:
                    up_ref[d, i] = jnp.where(low, re_turned, im).astype(jnp.bfloat16)
            return carry

        lax.fori_loop(0, GROUPS // 2, forward, 0, unroll=8)
        start_pair(edge_copies(d))
        if d == 0:

            def send_rest(o, carry):
                strip_copy(1, o).start()
                return carry

            lax.fori_loop(held, scene, send_rest, 0)
        focus_date(d)

    for big in range(GROUPS // 4):
        high = jnp.concatenate([high_ref[4 * big + j] for j in range(4)], axis=1)
        rest = jnp.concatenate([low_ref[4 * big + j] for j in range(4)], axis=1)
        looked = dot(high, look_ref[...]) + dot(rest, look_ref[...])
        own_ref[big] = looked[:, :LANES].astype(jnp.bfloat16)
        own_ref[HALO_CHUNKS + big] = looked[:, LANES:].astype(jnp.bfloat16)
    start_pair(look_copies())

    def lines_of(first_chunk, count):
        def forward_lines(step, carry):
            rows = []
            for j in range(4):
                chunk = first_chunk + 4 * step + j
                rows.append(
                    jnp.concatenate(
                        [line_ref[chunk, pl.ds(p, patches, stride=2)] for p in range(4)], axis=1
                    )
                )
            lines = jnp.concatenate(rows, axis=0).astype(jnp.bfloat16)
            result = dot(lines, azimuth_ref[...]).astype(jnp.bfloat16).astype(jnp.float32)
            for j in range(4):
                for r in range(4):
                    start = ((first_chunk + 4 * step + j) * 4 + r) * patches
                    grid_ref[pl.ds(pl.multiple_of(start, patches), patches)] = result[
                        j * patches : (j + 1) * patches, r * LANES : (r + 1) * LANES
                    ]
            return carry

        lax.fori_loop(0, count // 4, forward_lines, 0)

    for j in range(CHUNKS):
        line_ref[HALO_CHUNKS + j, pl.ds(1, SPLIT)] = own_ref[j].astype(jnp.float32)
    lines_of(HALO_CHUNKS, CHUNKS)
    wait_pair(look_copies())
    for j in range(HALO_CHUNKS):
        line_ref[j, pl.ds(1, SPLIT)] = own_before_ref[j].astype(jnp.float32)
        line_ref[HALO_CHUNKS + CHUNKS + j, pl.ds(1, SPLIT)] = own_after_ref[j].astype(jnp.float32)
    lines_of(0, HALO_CHUNKS)
    lines_of(HALO_CHUNKS + CHUNKS, HALO_CHUNKS)
    sign = jnp.where(low, 1.0, -1.0)

    def filter_patches(step, carry):
        tiles = []
        for j in range(4):
            tile = grid_ref[pl.ds(4 * step + j, PATCH, stride=patches)]
            swapped = pltpu.roll(tile, PATCH, 1) * sign
            tiles.append(jnp.concatenate([tile, swapped], axis=0).astype(jnp.bfloat16))
        spectra = dot(range_ref[...], jnp.concatenate(tiles, axis=1)) * (1.0 / PATCH)
        kept = []
        for j in range(4):
            spectrum = spectra[:, j * LANES : (j + 1) * LANES]
            power = spectrum * spectrum
            magnitude = jnp.sqrt(power + pltpu.roll(power, PATCH, 1) + EPSILON)
            row_sum = (
                magnitude
                + pltpu.roll(magnitude, 1, 0)
                + pltpu.roll(magnitude, PATCH - 1, 0)
            )
            smooth = (row_sum + pltpu.roll(row_sum, 1, 1) + pltpu.roll(row_sum, LANES - 1, 1)) * (
                1.0 / 9.0
            )
            level = jnp.sum(jnp.sum(magnitude, axis=0, keepdims=True), axis=1, keepdims=True)
            level = level * (1.0 / (PATCH * LANES)) + EPSILON
            kept.append((spectrum * (smooth / level)).astype(jnp.bfloat16))
        back = dot(jnp.concatenate(kept, axis=1), back_azimuth_ref[...]).astype(jnp.bfloat16)
        stacked = jnp.concatenate([back[:, :LANES], back[:, LANES:]], axis=0)
        result = (dot(back_range_ref[...], stacked) * (1.0 / PATCH)).astype(jnp.bfloat16)
        start = pl.multiple_of(step * LANES, LANES)
        out_ref[:, pl.ds(start, LANES)] = result
        return carry

    lax.fori_loop(0, patches // 4, filter_patches, 0, unroll=4)

    for d in range(dates):

        def sent(o, carry):
            strip_copy(d, o).wait_send()
            return carry

        lax.fori_loop(1, scene, sent, 0)


def loading_kernel(band_ref, *refs):
    held, out_ref, kept, load_sem = refs[:TABLES], refs[TABLES], refs[TABLES + 1 : -1], refs[-1]
    loads = [
        pltpu.make_async_copy(source, target, load_sem.at[i])
        for i, (source, target) in enumerate(zip(held, kept[:TABLES]))
    ]
    scene_kernel(band_ref, *kept[:TABLES], out_ref, *kept[TABLES:], loads)


def run_scene(raw, band, phase, left, scene, shape):
    dates, width = shape[1], shape[3]
    looks = SPLIT * SPLIT // LOOKS
    tc, ts = twiddle_tables()
    vmem = pl.BlockSpec(memory_space=pltpu.VMEM)
    plane = (GROUPS, SPLIT, LANES)
    edge = pltpu.VMEM((dates, SHIFT, SPLIT, LANES), jnp.bfloat16)
    looked_edge = pltpu.VMEM((HALO_CHUNKS, SPLIT, LANES), jnp.bfloat16)
    products = pltpu.VMEM((GROUPS, SPLIT, 2 * LANES), jnp.bfloat16)
    dma = pltpu.SemaphoreType.DMA
    tables = (
        raw, phase, bf16(left), bf16(spectrum_side(right_table(1.0), 1)),
        bf16(spectrum_side(right_table(-1.0), 0)), bf16(left_table(-1.0)),
        jnp.asarray(tc), jnp.asarray(ts), bf16(look_table()),
        bf16(patch_azimuth_table()), bf16(patch_range_table()),
        bf16(back_azimuth_table()), bf16(back_range_table()),
    )
    return pl.pallas_call(
        loading_kernel,
        in_specs=[pl.BlockSpec(memory_space=pltpu.SMEM)]
        + [pl.BlockSpec(memory_space=pl.ANY)] * TABLES,
        out_specs=vmem,
        out_shape=jax.ShapeDtypeStruct((2 * STRIP, looks), jnp.bfloat16),
        scratch_shapes=[pltpu.VMEM(table.shape, table.dtype) for table in tables]
        + [
            pltpu.VMEM(shape, jnp.bfloat16),
            pltpu.VMEM(raw.shape, jnp.float32),
            pltpu.VMEM((dates, scene, 2, STRIP, width), jnp.bfloat16),
            pltpu.VMEM((STRIP * SPLIT // 2, LANES), jnp.float32),
            pltpu.VMEM((2, pl.cdiv(width, LANES), scene * STRIP, LANES), jnp.float32),
            pltpu.VMEM((GROUPS, TAPS, SPLIT, LANES), jnp.float32),
            pltpu.VMEM(plane, jnp.float32),
            pltpu.VMEM(plane, jnp.float32),
            pltpu.VMEM((dates, 2, GROUPS + 2 * SHIFT, SPLIT, LANES), jnp.float32),
            edge, edge, edge, edge,
            pltpu.VMEM((GROUPS, 2 * SPLIT, LANES), jnp.bfloat16),
            products, products,
            pltpu.VMEM((CHUNKS, SPLIT, LANES), jnp.bfloat16),
            looked_edge,
            looked_edge,
            pltpu.VMEM((2 * CHUNKS, SPLIT + 8, LANES), jnp.float32),
            pltpu.VMEM((PATCH * SPLIT // 2, LANES), jnp.float32),
            dma((dates, scene)), dma((dates, scene)), dma((dates,)),
            dma((dates, 2)), dma((dates, 2)), dma((2,)), dma((2,)), dma((TABLES,)),
        ],
        compiler_params=pltpu.CompilerParams(
            vmem_limit_bytes=VMEM_LIMIT, collective_id=0, has_side_effects=True
        ),
        name="scene",
    )(band, *tables)


def on_device(raw_echoes, azimuth_phase, band_offset, partners):
    scene = lax.axis_size("scene")
    dates = raw_echoes.shape[2]
    local = raw_echoes.shape[0] // SPLIT
    pairs = partners.size
    assert dates == 2 and raw_echoes.shape[3] == scene * STRIP
    left = left_table(1.0).reshape(2 * SPLIT, 2, scene, local)
    left = left.transpose(0, 1, 3, 2).reshape(2 * SPLIT, 2 * SPLIT)
    lines, bins = raw_echoes.shape[0], raw_echoes.shape[3]
    raw = raw_echoes.reshape(lines, 2, dates, bins // LANES, LANES)
    raw = raw.transpose(0, 1, 3, 2, 4).reshape(-1, LANES)
    phase = azimuth_phase.T
    result = run_scene(
        raw, band_offset, phase, left, scene, (2, dates, bins, lines)
    )
    result = jnp.broadcast_to(result, (pairs,) + result.shape)
    return result.reshape(pairs, 2, STRIP, -1).transpose(0, 3, 1, 2)


def solution(mesh):
    return jax.shard_map(
        on_device,
        mesh=mesh,
        in_specs=(
            P("scene", None, "stack", None),
            P("stack", "scene"),
            P(("stack", "scene")),
            P("stack", None),
        ),
        out_specs=P("stack", None, None, "scene"),
        check_vma=False,
    )
```
